512 devices in a mesh: front: 128 (over x, z, core), chain: 4 (over y).
Axes of the slice: x: 4, y: 4, z: 16, core: 2. Of those that a mesh axis runs over, the one named last changes fastest.
Arguments:
- rhs: float32 [131072, 128], P(('front', 'chain')), may hold values from -6 to 6
- child_blocks: bfloat16 [45056, 128, 128], P(('front', 'chain')), may hold values from -4 to 4
- dest_front: int32 [45056, 1], P(('front', 'chain')), may hold values from 0 to 127; in each aligned block of 88 rows (0 to 87, 88 to 175, ...) at most 2 rows name the same one
- dest_place: int32 [45056], P(('front', 'chain')), may hold values from -4 to 23
- front_pivots: int32 [128], P('front'), may hold values from 512 to 1024, as said below
- diag_inv: float32 [131072, 256], P(('front', 'chain')), as said below
- lower_factor: bfloat16 [131072, 768], P(('front', 'chain')), may hold values from -0.1875 to 0.1875
- update_factor: bfloat16 [262144, 1024], P(('front', 'chain')), may hold values from -0.1875 to 0.1875
Outputs:
- solution: float32 [131072, 128], P(('front', 'chain'))
- update_out: float32 [262144, 128], P(('front', 'chain'))
The draws below stay inside these ranges and needn't reach their ends.
Inputs may be any that keep to these rules, and one draw needn't show every extreme that they name: `dest_front`: at most 2 of the 88 blocks of one device go to one front, and that many do in every draw. `front_pivots`: pivot rows at or beyond this count are padding and solve to zero; some front has all 1024. `diag_inv`: each 256 by 256 block is lower triangular with its diagonal between 0.4 and 1.6.
All inputs are finite; a program needn't handle non-finite values.
Results may differ from the reference program's by a relative error of at most 0.0027.
Values may be sent and summed in bfloat16 or wider, within the bound.
No kernel may reach another device: no remote copies, remote signals or barrier semaphores. Data moves between devices by JAX's collectives and lax.ppermute only.
A program may use at most 64 MiB of HBM per device.

```python
import math
import jax
import jax.numpy as jnp
import numpy as np
from jax import lax

P_SIZE = 1024
U = 2048
BR = 128
S = 128
CB = 88
FRONTS = 128
PB = 256
NBLK = 24
CBLOCKS = 45056
CAP = 2
N_CHAIN = 4


def draw_front_pivots(key, part):
    counts = jax.random.randint(key, (FRONTS,), P_SIZE // 2, P_SIZE + 1, dtype=jnp.int32)
    chosen = jax.random.randint(jax.random.fold_in(key, 7), (), 0, FRONTS, dtype=jnp.int32)
    return counts.at[chosen].set(P_SIZE)


def draw_diag_inv(key, part):
    block_rows = P_SIZE // N_CHAIN
    row_count = FRONTS * P_SIZE
    local_row = jnp.arange(row_count, dtype=jnp.int32)[:, None] % block_rows
    column = jnp.arange(block_rows, dtype=jnp.int32)[None, :]
    first_key, second_key = jax.random.split(key)
    diagonal = jax.random.uniform(first_key, (row_count, 1), jnp.float32, 0.6, 1.4)
    spread = jax.random.normal(second_key, (row_count, block_rows), jnp.float32) * (0.5 / jnp.sqrt(block_rows * 1.0))
    return jnp.where(local_row == column, diagonal, jnp.where(local_row > column, spread, 0.0)).astype(jnp.float32)


def plant(entries, stream_key, least, largest):
    extent = entries.shape
    place = [jax.random.randint(jax.random.fold_in(stream_key, axis), (), 0, extent[axis]) for axis in range(len(extent))]
    entries = entries.at[tuple(place)].set(least)
    longest = extent.index(max(extent))
    place[longest] = (place[longest] + 1) % extent[longest]
    return entries.at[tuple(place)].set(largest)


def level_of(key, dims, cuts, low, largest):
    gain, own = 1.0, jax.random.fold_in(key, 6)
    for axis_at, blocks in cuts:
        draws = jnp.exp(jax.random.uniform(jax.random.fold_in(own, axis_at), (blocks,), jnp.float32, low / len(cuts), largest / len(cuts)))
        gain = gain * jnp.repeat(draws, dims[axis_at] // blocks).reshape([-1 if axis == axis_at else 1 for axis in range(len(dims))])
    return gain


def routed_block(rng, own, number, rows, count, top, bound, lean):
    sequence = jax.random.permutation(rng, count)
    packed, usual = portions_of(count, rows * top, bound, lean, True), portions_of(count, rows * top, bound, lean, False)
    places = jnp.arange(count)

    def named(sizes, turn):
        used = int((sizes > 0).sum())
        fixed = max(1, used // 4)
        moved = fixed + (places - fixed + turn * (used - fixed)) % max(1, count - fixed)
        return jnp.zeros((count,), jnp.int32).at[sequence[jnp.where(places < fixed, places, moved)]].set(jnp.asarray(sizes, jnp.int32))

    sizes = jnp.where(number % 4 == 0, named(packed, number // 4), named(usual, number - number // 4 - 1))
    mixed = jax.random.permutation(jax.random.fold_in(own, 3), count)
    donor, sink = mixed[0:count // 2 * 2:2], mixed[1:count // 2 * 2:2]
    slack = jnp.minimum(sizes[donor] - 1, bound - sizes[sink]) // 2
    slack = jnp.where((donor == sequence[0]) | (sink == sequence[0]) | (sizes[sink] == 0), 0, jnp.maximum(slack, 0))
    moved = jax.random.randint(jax.random.fold_in(own, 4), (count // 2,), 0, 1 << 20) % (slack + 1)
    sizes = sizes.at[donor].add(-moved).at[sink].add(moved)
    items = jnp.searchsorted(jnp.cumsum(sizes), jnp.arange(rows * top), side="right").astype(jnp.int32)
    grid = items.reshape(top, rows).T
    grid = grid[jax.random.permutation(jax.random.fold_in(own, 1), rows)]
    turn = jax.random.randint(jax.random.fold_in(own, 2), (rows, 1), 0, top)
    return jnp.take_along_axis(grid, (jnp.arange(top)[None, :] + turn) % top, axis=1)


def portions_of(count, total, limit, lean, full):
    loads = [(1 << 20) // math.isqrt(rank ** lean) + 1 for rank in range(1, count + 1)]
    largest = limit if full else min(limit, max(-(-total // count), total * loads[0] // sum(loads)))
    least = 1 if total - largest >= count - 1 else 0
    given, surplus = [largest] + [least] * (count - 1), total - largest - least * (count - 1)
    while surplus > 0:
        candidates = [i for i in range(1, count) if given[i] < largest] or [i for i in range(1, count) if given[i] < limit]
        whole, left = sum([loads[i] for i in candidates]), surplus
        for i in candidates:
            addition = min(limit - given[i], max(1, left * loads[i] // whole), surplus)
            given[i] = given[i] + addition
            surplus = surplus - addition
    return np.array(given)


def scatter_about(key, extent, deviation, reach, cuts=(), kind=jnp.bfloat16):
    level = level_of(key, extent, cuts, -0.22, 0.18) if cuts else 1.0
    drawn = jax.random.normal(key, extent, jnp.float32) * deviation * level
    return jnp.minimum(jnp.maximum(drawn, -reach), reach).astype(kind)


def setup_inputs(seed: int = 0) -> dict:
    key_list = jax.random.split(jax.random.key(seed), 9)
    rhs = scatter_about(key_list[0], (FRONTS * P_SIZE, S), 1.0, 6.0, ((0, 512),), jnp.float32)
    child_blocks = scatter_about(key_list[1], (CBLOCKS, BR, S), 0.5, 4.0, ((0, 512),))
    dest_front_keys = jax.random.split(jax.random.fold_in(key_list[2], 1), CBLOCKS // CB)
    dest_front_turns = jax.random.permutation(jax.random.fold_in(key_list[2], 3), CBLOCKS // CB)
    dest_front = jax.vmap(lambda own, number: routed_block(jax.random.fold_in(key_list[2], 2), own, number, CB, FRONTS, 1, CAP, 2))(dest_front_keys, dest_front_turns).reshape((CBLOCKS, 1))
    dest_place = plant(jax.random.randint(key_list[3], (CBLOCKS,), -4, NBLK), jax.random.fold_in(key_list[3], 1), -4, NBLK - 1).astype(jnp.int32)
    front_pivots = draw_front_pivots(jax.random.fold_in(key_list[8], 71), 0)
    diag_inv = draw_diag_inv(jax.random.fold_in(key_list[8], 71), 0)
    lower_factor = scatter_about(key_list[6], (FRONTS * P_SIZE, P_SIZE - PB), P_SIZE ** -0.5, 0.1875, ((0, 512),))
    update_factor = scatter_about(key_list[7], (FRONTS * U, P_SIZE), P_SIZE ** -0.5, 0.1875, ((0, 512),))
    return {"rhs": rhs, "child_blocks": child_blocks, "dest_front": dest_front, "dest_place": dest_place, "front_pivots": front_pivots, "diag_inv": diag_inv, "lower_factor": lower_factor, "update_factor": update_factor}


def solve_front(inputs):
    pivot_rhs, update_rhs, count_live, inverse, lower, update = inputs
    live_rows = (jnp.arange(P_SIZE, dtype=jnp.int32) < count_live).astype(jnp.float32)[:, None]
    solved_list = []
    rounded_list = []
    for section in range(N_CHAIN):
        partial_value = pivot_rhs[section * PB:(section + 1) * PB]
        for earlier in range(section):
            factor_block = lower[section * PB:(section + 1) * PB, earlier * PB:(earlier + 1) * PB]
            partial_value = partial_value - jnp.dot(factor_block, rounded_list[earlier], preferred_element_type=jnp.float32)
        solved_here = live_rows[section * PB:(section + 1) * PB] * jnp.dot(inverse[section * PB:(section + 1) * PB], partial_value, precision=lax.Precision.HIGHEST)
        solved_list.append(solved_here)
        rounded_list.append(solved_here.astype(jnp.bfloat16))
    update_out = update_rhs - jnp.dot(update, jnp.concatenate(rounded_list, axis=0), preferred_element_type=jnp.float32)
    return jnp.concatenate(solved_list, axis=0), update_out


def reference(rhs, child_blocks, dest_front, dest_place, front_pivots, diag_inv, lower_factor, update_factor):
    slots_all = FRONTS * NBLK
    target = jnp.where(dest_place >= 0, dest_front[:, 0] * NBLK + dest_place, slots_all).astype(jnp.int32)
    holders = CBLOCKS // CB
    grouped = child_blocks.reshape(holders, CB, BR, S)
    grouped_target = target.reshape(holders, CB)

    def add_group(running, inputs):
        blocks_here, target_here = inputs
        return running.at[target_here].add(blocks_here.astype(jnp.float32)), None

    start = jnp.zeros((slots_all + 1, BR, S), jnp.float32)
    summed, _ = lax.scan(add_group, start, (grouped, grouped_target))
    assembled = summed[:slots_all].reshape(FRONTS, P_SIZE + U, S)
    pivot_all = rhs.reshape(FRONTS, P_SIZE, S) + assembled[:, :P_SIZE]
    solution, update_out = lax.map(solve_front, (pivot_all, assembled[:, P_SIZE:], front_pivots, diag_inv.reshape(FRONTS, P_SIZE, PB), lower_factor.reshape(FRONTS, P_SIZE, P_SIZE - PB), update_factor.reshape(FRONTS, U, P_SIZE)))
    return solution.reshape(FRONTS * P_SIZE, S), update_out.reshape(FRONTS * U, S)
```

```python
import jax
import jax.numpy as jnp
from jax import lax
from jax.experimental import pallas as pl
from jax.experimental.pallas import tpu as pltpu
from jax.sharding import Mesh, PartitionSpec as P

BR = 128
FRONT = ("x", "z", "core")
ALL = ("x", "z", "core", "chain")
SLAB = ("x", "core", "chain")
SLOTS = 11
PEERS = 32
LABEL_ROWS = 16
OWNED = 6


def slot_table(blocks, fronts, places, dest_count, slot_width):
    block_count = fronts.shape[0]
    sequence = jnp.arange(block_count, dtype=jnp.int32)
    earlier = (fronts[None, :] == fronts[:, None]) & (sequence[None, :] < sequence[:, None])
    rank_of = jnp.sum(earlier.astype(jnp.int32), axis=1)
    target = fronts * slot_width + rank_of
    source = jnp.full((dest_count * slot_width,), block_count, jnp.int32).at[target].set(sequence)
    slot_data = jnp.take(blocks, source, axis=0, mode="fill", fill_value=0)
    labels = jnp.take(places, source, axis=0, mode="fill", fill_value=-1)
    return (
        slot_data.reshape((dest_count, slot_width) + blocks.shape[1:]),
        labels.reshape(dest_count, slot_width),
    )


def full_exchange(child_blocks, fronts, places):
    slot_data, labels = slot_table(child_blocks, fronts, places, 128, 2)
    received = lax.all_to_all(slot_data, FRONT, split_axis=0, concat_axis=0, tiled=True)
    tags = lax.all_to_all(labels, FRONT, split_axis=0, concat_axis=0, tiled=True).reshape(-1)
    placed = jnp.where(
        tags < 8, tags // 2 * OWNED + tags % 2, (tags - 8) // 4 * OWNED + 2 + (tags - 8) % 4
    )
    placed = jnp.where(tags < 0, -1, placed)
    row_ids = jnp.arange(4 * OWNED, dtype=jnp.int32)
    onehot = (placed[None, :] == row_ids[:, None]).astype(jnp.bfloat16)
    flattened = received.reshape((-1,) + received.shape[2:])
    merged = jnp.einsum("km,mrs->krs", onehot, flattened, preferred_element_type=jnp.float32)
    return lax.psum_scatter(merged, "chain", scatter_dimension=0, tiled=True)


def send_kernel(front, place, blocks, out, over, marks, tags, counts, sem, tag_sem):
    for peer in range(PEERS):
        counts[peer] = 0
    marks[...] = jnp.full(marks.shape, -1.0, jnp.float32)
    lane = lax.broadcasted_iota(jnp.int32, (8, 128), 1)

    def step(i, carry):
        missed, sent = carry
        where_front = front[i]
        spot = place[i]
        live = spot >= 0
        pivot = spot < 8
        owner = jnp.where(pivot, spot >> 1, (spot - 8) >> 2)
        peer = ((where_front >> 5) * 2 + (where_front & 1)) * 4 + owner
        peer = jnp.where(live, peer, 0)
        index = ((where_front >> 1) & 15) * OWNED + jnp.where(pivot, spot & 1, 2 + ((spot - 8) & 3))
        used = counts[peer]
        fits = live & (used < SLOTS)

        @pl.when(fits)
        def _():
            counts[peer] = used + 1
            pltpu.make_async_copy(
                blocks.at[i], out.at[peer, pl.ds(pl.multiple_of(used * BR, BR), BR)], sem
            ).start()
            marks[peer] = jnp.where(lane == used, index.astype(jnp.float32), marks[peer])

        return (
            missed + jnp.where(live & (used >= SLOTS), 1, 0),
            sent + jnp.where(fits, 1, 0),
        )

    missed, sent = lax.fori_loop(0, front.shape[0], step, (jnp.int32(0), jnp.int32(0)))
    over[0] = missed
    half = marks[...].astype(jnp.bfloat16)
    tags[:, 0:8, :] = half
    tags[:, 8:16, :] = half
    tag_copy = pltpu.make_async_copy(tags, out.at[:, pl.ds(SLOTS * BR, LABEL_ROWS)], tag_sem)
    tag_copy.start()

    def drain(i, carry):
        pltpu.make_async_copy(blocks.at[0], out.at[0, pl.ds(0, BR)], sem).wait()
        return carry

    lax.fori_loop(0, sent, drain, 0)
    tag_copy.wait()


def pack(fronts, places, blocks):
    return pl.pallas_call(
        send_kernel,
        out_shape=(
            jax.ShapeDtypeStruct((PEERS, SLOTS * BR + LABEL_ROWS, 128), jnp.bfloat16),
            jax.ShapeDtypeStruct((1,), jnp.int32),
        ),
        in_specs=[
            pl.BlockSpec(memory_space=pltpu.SMEM),
            pl.BlockSpec(memory_space=pltpu.SMEM),
            pl.BlockSpec(memory_space=pl.ANY),
        ],
        out_specs=(pl.BlockSpec(memory_space=pl.ANY), pl.BlockSpec(memory_space=pltpu.SMEM)),
        scratch_shapes=[
            pltpu.VMEM((PEERS, 8, 128), jnp.float32),
            pltpu.VMEM((PEERS, LABEL_ROWS, 128), jnp.bfloat16),
            pltpu.SMEM((PEERS,), jnp.int32),
            pltpu.SemaphoreType.DMA,
            pltpu.SemaphoreType.DMA,
        ],
        name="pack",
    )(fronts, places, blocks)


def gather_kernel(index, block, out):
    source = pl.program_id(0)

    @pl.when(source == 0)
    def _():
        out[...] = jnp.zeros(out.shape, jnp.float32)

    for slot in range(SLOTS):
        target = index[source * SLOTS + slot]

        @pl.when(target >= 0)
        def _():
            out[target] += block[0, slot * BR : (slot + 1) * BR, :].astype(jnp.float32)


def add_up(index, received):
    rows = received.shape[1]
    return pl.pallas_call(
        gather_kernel,
        out_shape=jax.ShapeDtypeStruct((16 * OWNED, BR, 128), jnp.float32),
        grid_spec=pltpu.PrefetchScalarGridSpec(
            num_scalar_prefetch=1,
            grid=(PEERS,),
            in_specs=[pl.BlockSpec((1, rows, 128), lambda i, ids: (i, 0, 0))],
            out_specs=pl.BlockSpec((16 * OWNED, BR, 128), lambda i, ids: (0, 0, 0)),
        ),
        name="add_up",
    )(index, received)


def solve_kernel(spot, pivots, rhs, lower, inverse, owned, update, solved_out, update_out, kept):
    chain_at = spot[0]
    live_count = pivots[0]
    for block in range(4):
        rows = slice(block * 256, (block + 1) * 256)
        partial = rhs[rows, :]
        if block > 0:
            partial = partial - jnp.dot(
                lower[rows, 0 : block * 256],
                kept[0 : block * 256, :],
                preferred_element_type=jnp.float32,
            )
        row = block * 256 + lax.broadcasted_iota(jnp.int32, (256, 128), 0)
        product = jnp.dot(
            inverse[rows, :],
            partial,
            precision=lax.Precision.HIGHEST,
            preferred_element_type=jnp.float32,
        )
        here = jnp.where(row < live_count, product, 0.0)
        kept[rows, :] = here.astype(jnp.bfloat16)

        @pl.when(chain_at == block)
        def _():
            solved_out[...] = here

    update_out[...] = owned[256:768, :] - jnp.dot(
        update[...], kept[...], preferred_element_type=jnp.float32
    )


def solve(spot, pivots, rhs, lower, inverse, owned, update):
    smem = pl.BlockSpec(memory_space=pltpu.SMEM)
    vmem = pl.BlockSpec(memory_space=pltpu.VMEM)
    return pl.pallas_call(
        solve_kernel,
        out_shape=(
            jax.ShapeDtypeStruct((256, 128), jnp.float32),
            jax.ShapeDtypeStruct((512, 128), jnp.float32),
        ),
        in_specs=[smem, smem, vmem, vmem, vmem, vmem, vmem],
        out_specs=(vmem, vmem),
        scratch_shapes=[pltpu.VMEM((1024, 128), jnp.bfloat16)],
        name="solve",
    )(spot, pivots, rhs, lower, inverse, owned, update)


def body(
    rhs, child_blocks, dest_front, dest_place, front_pivots, diag_inv, lower_factor, update_factor
):
    fronts = dest_front.reshape(-1)
    packed, over = pack(fronts, dest_place, child_blocks)
    overflow = lax.pmax(over, ALL)
    received = lax.all_to_all(packed, SLAB, split_axis=0, concat_axis=0, tiled=True)
    index = received[:, SLOTS * BR, :SLOTS].astype(jnp.int32).reshape(-1)
    dense = add_up(index, received)
    owned = lax.psum_scatter(dense, "z", scatter_dimension=0, tiled=True)
    owned = lax.cond(
        overflow[0] > 0,
        lambda fast: full_exchange(child_blocks, fronts, dest_place),
        lambda fast: fast,
        owned,
    )
    owned = owned.reshape(OWNED * BR, 128)
    all_lower = lax.all_gather(lower_factor, "chain", axis=0, tiled=True)
    all_inverse = lax.all_gather(diag_inv, "chain", axis=0, tiled=True)
    all_rhs = lax.all_gather(rhs + owned[:256], "chain", axis=0, tiled=True)
    spot = lax.axis_index("chain").astype(jnp.int32).reshape(1)
    return solve(spot, front_pivots, all_rhs, all_lower, all_inverse, owned, update_factor)


def solution(mesh):
    grid = Mesh(mesh.devices.reshape(4, 16, 2, 4), ALL)
    rows = P(ALL, None)
    return jax.shard_map(
        body,
        mesh=grid,
        in_specs=(rows, P(ALL, None, None), rows, P(ALL), P(FRONT), rows, rows, rows),
        out_specs=(rows, rows),
        check_vma=False,
    )
```

```python
import jax
import jax.numpy as jnp
from jax import lax
from jax.experimental import pallas as pl
from jax.experimental.pallas import tpu as pltpu
from jax.sharding import Mesh, PartitionSpec as P

BR = 128
FRONT = ("x", "z", "core")
ALL = ("x", "z", "core", "chain")
SLAB = ("x", "core", "chain")
SLOTS = 11
PEERS = 32
LABEL_ROWS = 16
OWNED = 6
COUNT_LANE = 126
OVER_LANE = 127
CHUNK = OWNED * BR + 8


def slot_table(blocks, fronts, places, dest_count, slot_width):
    block_count = fronts.shape[0]
    sequence = jnp.arange(block_count, dtype=jnp.int32)
    earlier = (fronts[None, :] == fronts[:, None]) & (sequence[None, :] < sequence[:, None])
    rank_of = jnp.sum(earlier.astype(jnp.int32), axis=1)
    target = fronts * slot_width + rank_of
    source = jnp.full((dest_count * slot_width,), block_count, jnp.int32).at[target].set(sequence)
    slot_data = jnp.take(blocks, source, axis=0, mode="fill", fill_value=0)
    labels = jnp.take(places, source, axis=0, mode="fill", fill_value=-1)
    return (
        slot_data.reshape((dest_count, slot_width) + blocks.shape[1:]),
        labels.reshape(dest_count, slot_width),
    )


def full_exchange(child_blocks, fronts, places):
    slot_data, labels = slot_table(child_blocks, fronts, places, 128, 2)
    received = lax.all_to_all(slot_data, FRONT, split_axis=0, concat_axis=0, tiled=True)
    tags = lax.all_to_all(labels, FRONT, split_axis=0, concat_axis=0, tiled=True).reshape(-1)
    placed = jnp.where(
        tags < 8, tags // 2 * OWNED + tags % 2, (tags - 8) // 4 * OWNED + 2 + (tags - 8) % 4
    )
    placed = jnp.where(tags < 0, -1, placed)
    row_ids = jnp.arange(4 * OWNED, dtype=jnp.int32)
    onehot = (placed[None, :] == row_ids[:, None]).astype(jnp.bfloat16)
    flattened = received.reshape((-1,) + received.shape[2:])
    merged = jnp.einsum("km,mrs->krs", onehot, flattened, preferred_element_type=jnp.float32)
    return lax.psum_scatter(merged, "chain", scatter_dimension=0, tiled=True)


def send_kernel(front, place, blocks, out, marks, tags, counts, sem, tag_sem):
    for peer in range(PEERS):
        counts[peer] = 0
    marks[...] = jnp.full(marks.shape, -1.0, jnp.float32)
    lane = lax.broadcasted_iota(jnp.int32, (8, 128), 1)

    def step(i, carry):
        missed, sent = carry
        where_front = front[i]
        spot = place[i]
        live = spot >= 0
        pivot = spot < 8
        owner = jnp.where(pivot, spot >> 1, (spot - 8) >> 2)
        peer = ((where_front >> 5) * 2 + (where_front & 1)) * 4 + owner
        peer = jnp.where(live, peer, 0)
        index = ((where_front >> 1) & 15) * OWNED + jnp.where(pivot, spot & 1, 2 + ((spot - 8) & 3))
        used = counts[peer]
        fits = live & (used < SLOTS)

        @pl.when(fits)
        def _():
            counts[peer] = used + 1
            pltpu.make_async_copy(
                blocks.at[i], out.at[peer, pl.ds(pl.multiple_of(used * BR, BR), BR)], sem
            ).start()
            marks[peer] = jnp.where(lane == used, index.astype(jnp.float32), marks[peer])

        return (
            missed + jnp.where(live & (used >= SLOTS), 1, 0),
            sent + jnp.where(fits, 1, 0),
        )

    missed, sent = lax.fori_loop(0, front.shape[0], step, (jnp.int32(0), jnp.int32(0)))
    for peer in range(PEERS):
        row = jnp.where(lane == COUNT_LANE, counts[peer].astype(jnp.float32), marks[peer])
        row = jnp.where(lane == OVER_LANE, missed.astype(jnp.float32), row)
        tags[peer, 0:8, :] = row.astype(jnp.bfloat16)
        tags[peer, 8:16, :] = row.astype(jnp.bfloat16)
    tag_copy = pltpu.make_async_copy(tags, out.at[:, pl.ds(SLOTS * BR, LABEL_ROWS)], tag_sem)
    tag_copy.start()

    def drain(i, carry):
        pltpu.make_async_copy(blocks.at[0], out.at[0, pl.ds(0, BR)], sem).wait()
        return carry

    lax.fori_loop(0, sent, drain, 0)
    tag_copy.wait()


def pack(fronts, places, blocks):
    return pl.pallas_call(
        send_kernel,
        out_shape=jax.ShapeDtypeStruct((PEERS, SLOTS * BR + LABEL_ROWS, 128), jnp.bfloat16),
        in_specs=[
            pl.BlockSpec(memory_space=pltpu.SMEM),
            pl.BlockSpec(memory_space=pltpu.SMEM),
            pl.BlockSpec(memory_space=pltpu.VMEM),
        ],
        out_specs=pl.BlockSpec(memory_space=pl.ANY),
        scratch_shapes=[
            pltpu.VMEM((PEERS, 8, 128), jnp.float32),
            pltpu.VMEM((PEERS, LABEL_ROWS, 128), jnp.bfloat16),
            pltpu.SMEM((PEERS,), jnp.int32),
            pltpu.SemaphoreType.DMA,
            pltpu.SemaphoreType.DMA,
        ],
        name="pack",
    )(fronts, places, blocks)


def gather_kernel(index, received, out, total, landed, sems, sem):
    def fetch(i, at):
        def slot(j, spot):
            pltpu.make_async_copy(
                received.at[i, pl.ds(pl.multiple_of(j * BR, BR), BR)], landed.at[spot], sems.at[i]
            ).start()
            return spot + 1

        return lax.fori_loop(0, index[i, 0, COUNT_LANE], slot, at)

    lax.fori_loop(0, PEERS, fetch, jnp.int32(0))
    total[...] = jnp.zeros(total.shape, jnp.float32)

    def source(i, carry):
        missed, at = carry
        count = index[i, 0, COUNT_LANE]

        def arrive(j, carry):
            pltpu.make_async_copy(received.at[0, pl.ds(0, BR)], landed.at[0], sems.at[i]).wait()
            return carry

        lax.fori_loop(0, count, arrive, 0)

        def slot(j, spot):
            target = index[i, 0, j]
            chunk = target // OWNED
            start = pl.multiple_of((target - chunk * OWNED) * BR, BR)
            total[chunk, pl.ds(start, BR), :] += landed[spot].astype(jnp.float32)
            return spot + 1

        at = lax.fori_loop(0, count, slot, at)
        return missed + index[i, 0, OVER_LANE], at

    missed, _ = lax.fori_loop(0, PEERS, source, (jnp.int32(0), jnp.int32(0)))
    total[:, OWNED * BR :, :] = jnp.full((16, 8, 128), missed.astype(jnp.float32))
    copy = pltpu.make_async_copy(total, out, sem)
    copy.start()
    copy.wait()


def add_up(index, received):
    return pl.pallas_call(
        gather_kernel,
        out_shape=jax.ShapeDtypeStruct((16, CHUNK, 128), jnp.float32),
        in_specs=[
            pl.BlockSpec(memory_space=pltpu.SMEM),
            pl.BlockSpec(memory_space=pl.ANY),
        ],
        out_specs=pl.BlockSpec(memory_space=pl.ANY),
        scratch_shapes=[
            pltpu.VMEM((16, CHUNK, 128), jnp.float32),
            pltpu.VMEM((PEERS * SLOTS, BR, 128), jnp.bfloat16),
            pltpu.SemaphoreType.DMA((PEERS,)),
            pltpu.SemaphoreType.DMA,
        ],
        name="add_up",
    )(index, received)


def solve_kernel(spot, pivots, rhs, *refs):
    lowers, inverses = refs[0:4], refs[4:8]
    owned, update, solved_out, update_out, lower, inverse, kept = refs[8:]
    chain_at = spot[0]
    live_count = pivots[0]
    for shift in range(4):
        block = (chain_at - shift) & 3
        lower[block] = lowers[shift][...]
        inverse[block] = inverses[shift][...]
    for block in range(4):
        rows = slice(block * 256, (block + 1) * 256)
        partial = rhs[rows, :]
        if block > 0:
            partial = partial - jnp.dot(
                lower[block, :, 0 : block * 256],
                kept[0 : block * 256, :],
                preferred_element_type=jnp.float32,
            )
        row = block * 256 + lax.broadcasted_iota(jnp.int32, (256, 128), 0)
        product = jnp.dot(
            inverse[block],
            partial,
            precision=lax.Precision.HIGHEST,
            preferred_element_type=jnp.float32,
        )
        here = jnp.where(row < live_count, product, 0.0)
        kept[rows, :] = here.astype(jnp.bfloat16)

        @pl.when(chain_at == block)
        def _():
            solved_out[...] = here

    update_out[...] = owned[256:768, :] - jnp.dot(
        update[...], kept[...], preferred_element_type=jnp.float32
    )


def solve(spot, pivots, rhs, lowers, inverses, owned, update):
    smem = pl.BlockSpec(memory_space=pltpu.SMEM)
    vmem = pl.BlockSpec(memory_space=pltpu.VMEM)
    return pl.pallas_call(
        solve_kernel,
        out_shape=(
            jax.ShapeDtypeStruct((256, 128), jnp.float32),
            jax.ShapeDtypeStruct((512, 128), jnp.float32),
        ),
        in_specs=[smem, smem] + [vmem] * 11,
        out_specs=(vmem, vmem),
        scratch_shapes=[
            pltpu.VMEM((4, 256, 768), jnp.bfloat16),
            pltpu.VMEM((4, 256, 256), jnp.float32),
            pltpu.VMEM((1024, 128), jnp.bfloat16),
        ],
        name="solve",
    )(spot, pivots, rhs, *lowers, *inverses, owned, update)


def around_chain(value):
    moved = [
        lax.ppermute(value, "chain", [(i, (i + shift) % 4) for i in range(4)])
        for shift in (1, 2, 3)
    ]
    return (value, *moved)


def body(
    rhs, child_blocks, dest_front, dest_place, front_pivots, diag_inv, lower_factor, update_factor
):
    fronts = dest_front.reshape(-1)
    packed = pack(fronts, dest_place, child_blocks)
    received = lax.all_to_all(packed, SLAB, split_axis=0, concat_axis=0, tiled=True)
    index = received[:, SLOTS * BR : SLOTS * BR + 1, :].astype(jnp.int32)
    dense = add_up(index, received)
    dense, lower_factor, diag_inv = lax.optimization_barrier((dense, lower_factor, diag_inv))
    owned = lax.psum_scatter(dense, "z", scatter_dimension=0, tiled=True).reshape(CHUNK, 128)
    lowers = around_chain(lower_factor)
    inverses = around_chain(diag_inv)
    spot = lax.axis_index("chain").astype(jnp.int32).reshape(1)

    def finish(mine):
        all_rhs = lax.all_gather(rhs + mine[:256], "chain", axis=0, tiled=True)
        return solve(spot, front_pivots, all_rhs, lowers, inverses, mine, update_factor)

    def general(mine):
        exchanged = full_exchange(child_blocks, fronts, dest_place)
        return finish(jnp.concatenate([exchanged.reshape(OWNED * BR, 128), mine[OWNED * BR :]]))

    return lax.cond(owned[OWNED * BR, 0] > 0, general, finish, owned)


def solution(mesh):
    grid = Mesh(mesh.devices.reshape(4, 16, 2, 4), ALL)
    rows = P(ALL, None)
    return jax.shard_map(
        body,
        mesh=grid,
        in_specs=(rows, P(ALL, None, None), rows, P(ALL), P(FRONT), rows, rows, rows),
        out_specs=(rows, rows),
        check_vma=False,
    )
```

```python
import jax
import jax.numpy as jnp
from jax import lax
from jax.experimental import pallas as pl
from jax.experimental.pallas import tpu as pltpu
from jax.sharding import Mesh, PartitionSpec as P

BR = 128
FRONT = ("x", "z", "core")
ALL = ("x", "z", "core", "chain")
SLAB = ("x", "core", "chain")
LINE = ("x", "core")
SLOTS = 5
HOPS = 6
PEERS = 32
GROUPS = 8
LABEL_ROWS = 16
OWNED = 6
HOP_LANE = 64
STRAY_LANE = 125
COUNT_LANE = 126
OVER_LANE = 127
PIVOT_ROWS = 256
FLAG_ROWS = 8
CHUNK = OWNED * BR + FLAG_ROWS


def slot_table(blocks, fronts, places, dest_count, slot_width):
    block_count = fronts.shape[0]
    sequence = jnp.arange(block_count, dtype=jnp.int32)
    earlier = (fronts[None, :] == fronts[:, None]) & (sequence[None, :] < sequence[:, None])
    rank_of = jnp.sum(earlier.astype(jnp.int32), axis=1)
    target = fronts * slot_width + rank_of
    source = jnp.full((dest_count * slot_width,), block_count, jnp.int32).at[target].set(sequence)
    slot_data = jnp.take(blocks, source, axis=0, mode="fill", fill_value=0)
    labels = jnp.take(places, source, axis=0, mode="fill", fill_value=-1)
    return (
        slot_data.reshape((dest_count, slot_width) + blocks.shape[1:]),
        labels.reshape(dest_count, slot_width),
    )


def full_exchange(child_blocks, fronts, places):
    slot_data, labels = slot_table(child_blocks, fronts, places, 128, 2)
    received = lax.all_to_all(slot_data, FRONT, split_axis=0, concat_axis=0, tiled=True)
    tags = lax.all_to_all(labels, FRONT, split_axis=0, concat_axis=0, tiled=True).reshape(-1)
    placed = jnp.where(
        tags < 8, tags // 2 * OWNED + tags % 2, (tags - 8) // 4 * OWNED + 2 + (tags - 8) % 4
    )
    placed = jnp.where(tags < 0, -1, placed)
    row_ids = jnp.arange(4 * OWNED, dtype=jnp.int32)
    onehot = (placed[None, :] == row_ids[:, None]).astype(jnp.bfloat16)
    flattened = received.reshape((-1,) + received.shape[2:])
    merged = jnp.einsum("km,mrs->krs", onehot, flattened, preferred_element_type=jnp.float32)
    return lax.psum_scatter(merged, "chain", scatter_dimension=0, tiled=True)


def write_tags(marks, tags, counts, strays, missed, count):
    lane = lax.broadcasted_iota(jnp.int32, (8, 128), 1)
    for peer in range(count):
        row = jnp.where(lane == COUNT_LANE, counts[peer].astype(jnp.float32), marks[peer])
        if strays is not None:
            row = jnp.where(lane == STRAY_LANE, strays[peer].astype(jnp.float32), row)
        row = jnp.where(lane == OVER_LANE, missed.astype(jnp.float32), row)
        tags[peer, 0:8, :] = row.astype(jnp.bfloat16)
        tags[peer, 8:16, :] = row.astype(jnp.bfloat16)


def send_kernel(spot, front, place, blocks, out, marks, tags, counts, strays, late, sem, tag_sem):
    for peer in range(PEERS):
        counts[peer] = 0
        strays[peer] = 0
    marks[...] = jnp.full(marks.shape, -1.0, jnp.float32)
    lane = lax.broadcasted_iota(jnp.int32, (8, 128), 1)

    def route(i):
        where_front = front[i]
        target = place[i]
        pivot = target < 8
        owner = jnp.where(pivot, target >> 1, (target - 8) >> 2)
        peer = ((where_front >> 5) * 2 + (where_front & 1)) * 4 + owner
        index = ((where_front >> 1) & 15) * OWNED + jnp.where(
            pivot, target & 1, 2 + ((target - 8) & 3)
        )
        live = target >= 0
        return live, jnp.where(live, peer, 0), index

    def launch(i, peer, used):
        pltpu.make_async_copy(
            blocks.at[i], out.at[peer, pl.ds(pl.multiple_of(used * BR, BR), BR)], sem
        ).start()

    def direct(i, carry):
        left, sent = carry
        live, peer, index = route(i)
        used = counts[peer]
        fits = live & (used < SLOTS)

        @pl.when(fits)
        def _():
            counts[peer] = used + 1
            launch(i, peer, used)
            marks[peer] = jnp.where(lane == used, index.astype(jnp.float32), marks[peer])

        @pl.when(live & (used >= SLOTS))
        def _():
            late[left] = i

        return (
            left + jnp.where(live & (used >= SLOTS), 1, 0),
            sent + jnp.where(fits, 1, 0),
        )

    left, sent = lax.fori_loop(0, front.shape[0], direct, (jnp.int32(0), jnp.int32(0)))

    def detour(k, carry):
        missed, sent = carry
        i = late[k]
        _, home, index = route(i)
        group = home >> 2
        chosen = jnp.int32(-1)
        for h in reversed(range(GROUPS - 1)):
            turn = lax.rem(spot[0] + k + h, GROUPS - 1)
            peer = (((group + 1 + turn) & 7) << 2) + (home & 3)
            chosen = jnp.where(counts[peer] < SLOTS, peer, chosen)
        fits = chosen >= 0

        @pl.when(fits)
        def _():
            used = counts[chosen]
            counts[chosen] = used + 1
            strays[chosen] = strays[chosen] + 1
            launch(i, chosen, used)
            row = jnp.where(lane == used, index.astype(jnp.float32), marks[chosen])
            marks[chosen] = jnp.where(lane == HOP_LANE + used, group.astype(jnp.float32), row)

        return missed + jnp.where(fits, 0, 1), sent + jnp.where(fits, 1, 0)

    missed, sent = lax.fori_loop(0, left, detour, (jnp.int32(0), sent))
    write_tags(marks, tags, counts, strays, missed, PEERS)
    tag_copy = pltpu.make_async_copy(tags, out.at[:, pl.ds(SLOTS * BR, LABEL_ROWS)], tag_sem)
    tag_copy.start()

    def drain(i, carry):
        pltpu.make_async_copy(blocks.at[0], out.at[0, pl.ds(0, BR)], sem).wait()
        return carry

    lax.fori_loop(0, sent, drain, 0)
    tag_copy.wait()


def pack(turn, fronts, places, blocks):
    smem = pl.BlockSpec(memory_space=pltpu.SMEM)
    return pl.pallas_call(
        send_kernel,
        out_shape=jax.ShapeDtypeStruct((PEERS, SLOTS * BR + LABEL_ROWS, 128), jnp.bfloat16),
        in_specs=[smem, smem, smem, pl.BlockSpec(memory_space=pltpu.VMEM)],
        out_specs=pl.BlockSpec(memory_space=pl.ANY),
        scratch_shapes=[
            pltpu.VMEM((PEERS, 8, 128), jnp.float32),
            pltpu.VMEM((PEERS, LABEL_ROWS, 128), jnp.bfloat16),
            pltpu.SMEM((PEERS,), jnp.int32),
            pltpu.SMEM((PEERS,), jnp.int32),
            pltpu.SMEM((128,), jnp.int32),
            pltpu.SemaphoreType.DMA,
            pltpu.SemaphoreType.DMA,
        ],
        compiler_params=pltpu.CompilerParams(vmem_limit_bytes=8 << 20),
        name="pack",
    )(turn, fronts, places, blocks)


def forward_kernel(index, received, out, marks, tags, counts, sem, tag_sem):
    for peer in range(GROUPS):
        counts[peer] = 0
    marks[...] = jnp.full(marks.shape, -1.0, jnp.float32)
    lane = lax.broadcasted_iota(jnp.int32, (8, 128), 1)

    def source(i, carry):
        def slot(j, carry):
            missed, sent = carry
            home = index[i, 0, HOP_LANE + j]
            stray = home >= 0
            used = counts[jnp.maximum(home, 0)]
            fits = stray & (used < HOPS)

            @pl.when(fits)
            def _():
                counts[home] = used + 1
                pltpu.make_async_copy(
                    received.at[i, pl.ds(pl.multiple_of(j * BR, BR), BR)],
                    out.at[home, pl.ds(pl.multiple_of(used * BR, BR), BR)],
                    sem,
                ).start()
                target = index[i, 0, j].astype(jnp.float32)
                marks[home] = jnp.where(lane == used, target, marks[home])

            return (
                missed + jnp.where(stray & (used >= HOPS), 1, 0),
                sent + jnp.where(fits, 1, 0),
            )

        count = jnp.where(index[i, 0, STRAY_LANE] > 0, index[i, 0, COUNT_LANE], 0)
        return lax.fori_loop(0, count, slot, carry)

    missed, sent = lax.fori_loop(0, PEERS, source, (jnp.int32(0), jnp.int32(0)))
    write_tags(marks, tags, counts, None, missed, GROUPS)
    tag_copy = pltpu.make_async_copy(tags, out.at[:, pl.ds(HOPS * BR, LABEL_ROWS)], tag_sem)
    tag_copy.start()

    def drain(i, carry):
        pltpu.make_async_copy(received.at[0, pl.ds(0, BR)], out.at[0, pl.ds(0, BR)], sem).wait()
        return carry

    lax.fori_loop(0, sent, drain, 0)
    tag_copy.wait()


def forward(index, received):
    return pl.pallas_call(
        forward_kernel,
        out_shape=jax.ShapeDtypeStruct((GROUPS, HOPS * BR + LABEL_ROWS, 128), jnp.bfloat16),
        in_specs=[
            pl.BlockSpec(memory_space=pltpu.SMEM),
            pl.BlockSpec(memory_space=pl.ANY),
        ],
        out_specs=pl.BlockSpec(memory_space=pl.ANY),
        scratch_shapes=[
            pltpu.VMEM((GROUPS, 8, 128), jnp.float32),
            pltpu.VMEM((GROUPS, LABEL_ROWS, 128), jnp.bfloat16),
            pltpu.SMEM((GROUPS,), jnp.int32),
            pltpu.SemaphoreType.DMA,
            pltpu.SemaphoreType.DMA,
        ],
        compiler_params=pltpu.CompilerParams(vmem_limit_bytes=2 << 20),
        name="forward",
    )(index, received)


def gather_kernel(index, late_index, received, late, out, total, landed, sems, sem):
    def fetch_from(array, labels, first):
        def fetch(i, at):
            def slot(j, spot):
                pltpu.make_async_copy(
                    array.at[i, pl.ds(pl.multiple_of(j * BR, BR), BR)],
                    landed.at[spot],
                    sems.at[first + i],
                ).start()
                return spot + 1

            return lax.fori_loop(0, labels[i, 0, COUNT_LANE], slot, at)

        return fetch

    def add_from(array, labels, first):
        def source(i, carry):
            missed, at = carry
            count = labels[i, 0, COUNT_LANE]

            def arrive(j, carry):
                pltpu.make_async_copy(
                    array.at[0, pl.ds(0, BR)], landed.at[0], sems.at[first + i]
                ).wait()
                return carry

            lax.fori_loop(0, count, arrive, 0)

            def slot(j, spot):
                target = labels[i, 0, j]
                chunk = target // OWNED
                row = target - chunk * OWNED
                start = row * BR + jnp.where(row >= 2, FLAG_ROWS, 0)
                chunk = jnp.where(labels[i, 0, HOP_LANE + j] >= 0, 16, chunk)
                start = pl.multiple_of(start, 8)
                total[chunk, pl.ds(start, BR), :] += landed[spot].astype(jnp.float32)
                return spot + 1

            at = lax.fori_loop(0, count, slot, at)
            return missed + labels[i, 0, OVER_LANE], at

        return source

    at = lax.fori_loop(0, PEERS, fetch_from(received, index, 0), jnp.int32(0))
    lax.fori_loop(0, GROUPS, fetch_from(late, late_index, PEERS), at)
    total[0:16] = jnp.zeros((16, CHUNK, 128), jnp.float32)
    carry = (jnp.int32(0), jnp.int32(0))
    carry = lax.fori_loop(0, PEERS, add_from(received, index, 0), carry)
    missed, _ = lax.fori_loop(0, GROUPS, add_from(late, late_index, PEERS), carry)
    total[0:16, PIVOT_ROWS : PIVOT_ROWS + FLAG_ROWS, :] = jnp.full(
        (16, FLAG_ROWS, 128), missed.astype(jnp.float32)
    )
    copy = pltpu.make_async_copy(total.at[pl.ds(0, 16)], out, sem)
    copy.start()
    copy.wait()


def add_up(index, late_index, received, late):
    smem = pl.BlockSpec(memory_space=pltpu.SMEM)
    anywhere = pl.BlockSpec(memory_space=pl.ANY)
    return pl.pallas_call(
        gather_kernel,
        out_shape=jax.ShapeDtypeStruct((16, CHUNK, 128), jnp.float32),
        in_specs=[smem, smem, anywhere, anywhere],
        out_specs=anywhere,
        scratch_shapes=[
            pltpu.VMEM((17, CHUNK, 128), jnp.float32),
            pltpu.VMEM((PEERS * SLOTS + GROUPS * HOPS, BR, 128), jnp.bfloat16),
            pltpu.SemaphoreType.DMA((PEERS + GROUPS,)),
            pltpu.SemaphoreType.DMA,
        ],
        compiler_params=pltpu.CompilerParams(vmem_limit_bytes=20 << 20),
        name="add_up",
    )(index, late_index, received, late)


def solve_kernel(spot, pivots, rhs, *refs):
    lowers, inverses = refs[0:4], refs[4:8]
    owned, update, solved_out, update_out, lower, inverse, kept = refs[8:]
    chain_at = spot[0]
    live_count = pivots[0]
    for shift in range(4):
        block = (chain_at - shift) & 3
        lower[block] = lowers[shift][...]
        inverse[block] = inverses[shift][...]
    for block in range(4):
        rows = slice(block * 256, (block + 1) * 256)
        at = block * (PIVOT_ROWS + FLAG_ROWS)
        partial = rhs[at : at + PIVOT_ROWS, :]
        if block > 0:
            partial = partial - jnp.dot(
                lower[block, :, 0 : block * 256],
                kept[0 : block * 256, :],
                preferred_element_type=jnp.float32,
            )
        row = block * 256 + lax.broadcasted_iota(jnp.int32, (256, 128), 0)
        product = jnp.dot(
            inverse[block],
            partial,
            precision=lax.Precision.HIGHEST,
            preferred_element_type=jnp.float32,
        )
        here = jnp.where(row < live_count, product, 0.0)
        kept[rows, :] = here.astype(jnp.bfloat16)

        @pl.when(chain_at == block)
        def _():
            solved_out[...] = here

    update_out[...] = owned[PIVOT_ROWS + FLAG_ROWS :, :] - jnp.dot(
        update[...], kept[...], preferred_element_type=jnp.float32
    )


def solve(spot, pivots, rhs, lowers, inverses, owned, update):
    smem = pl.BlockSpec(memory_space=pltpu.SMEM)
    vmem = pl.BlockSpec(memory_space=pltpu.VMEM)
    return pl.pallas_call(
        solve_kernel,
        out_shape=(
            jax.ShapeDtypeStruct((256, 128), jnp.float32),
            jax.ShapeDtypeStruct((512, 128), jnp.float32),
        ),
        in_specs=[smem, smem] + [vmem] * 11,
        out_specs=(vmem, vmem),
        scratch_shapes=[
            pltpu.VMEM((4, 256, 768), jnp.bfloat16),
            pltpu.VMEM((4, 256, 256), jnp.float32),
            pltpu.VMEM((1024, 128), jnp.bfloat16),
        ],
        compiler_params=pltpu.CompilerParams(vmem_limit_bytes=20 << 20),
        name="solve",
    )(spot, pivots, rhs, *lowers, *inverses, owned, update)


def around_chain(value):
    moved = [
        lax.ppermute(value, "chain", [(i, (i + shift) % 4) for i in range(4)])
        for shift in (1, 2, 3)
    ]
    return (value, *moved)


def labels_of(received):
    return received[:, -LABEL_ROWS : 1 - LABEL_ROWS, :].astype(jnp.int32)


def body(
    rhs, child_blocks, dest_front, dest_place, front_pivots, diag_inv, lower_factor, update_factor
):
    fronts = dest_front.reshape(-1)
    spot = lax.axis_index("chain").astype(jnp.int32).reshape(1)
    turn = lax.axis_index(LINE).astype(jnp.int32).reshape(1) + 2 * spot
    packed = pack(turn, fronts, dest_place, child_blocks)
    received = lax.all_to_all(packed, SLAB, split_axis=0, concat_axis=0, tiled=True)
    index = labels_of(received)
    late = lax.all_to_all(forward(index, received), LINE, split_axis=0, concat_axis=0, tiled=True)
    dense = add_up(index, labels_of(late), received, late)
    dense, lower_factor, diag_inv = lax.optimization_barrier((dense, lower_factor, diag_inv))
    owned = lax.psum_scatter(dense, "z", scatter_dimension=0, tiled=True)
    owned = lax.optimization_barrier(owned).reshape(CHUNK, 128)
    lowers = around_chain(lower_factor)
    inverses = around_chain(diag_inv)

    def share(mine):
        padded = jnp.pad(rhs, ((0, FLAG_ROWS), (0, 0)))
        return lax.all_gather(
            padded + mine[: PIVOT_ROWS + FLAG_ROWS], "chain", axis=0, tiled=True
        )

    def finish(all_rhs, mine):
        return solve(spot, front_pivots, all_rhs, lowers, inverses, mine, update_factor)

    def general(all_rhs, mine):
        blocks = full_exchange(child_blocks, fronts, dest_place).reshape(OWNED * BR, 128)
        flags = jnp.zeros((FLAG_ROWS, 128), jnp.float32)
        mine = jnp.concatenate([blocks[:PIVOT_ROWS], flags, blocks[PIVOT_ROWS:]])
        return finish(share(mine), mine)

    all_rhs = share(owned)
    over = jnp.sum(all_rhs.reshape(4, PIVOT_ROWS + FLAG_ROWS, 128)[:, PIVOT_ROWS, 0])
    return lax.cond(over > 0, general, finish, all_rhs, owned)


def solution(mesh):
    grid = Mesh(mesh.devices.reshape(4, 16, 2, 4), ALL)
    rows = P(ALL, None)
    return jax.shard_map(
        body,
        mesh=grid,
        in_specs=(rows, P(ALL, None, None), rows, P(ALL), P(FRONT), rows, rows, rows),
        out_specs=(rows, rows),
        check_vma=False,
    )
```

```python
import jax
import jax.numpy as jnp
from jax import lax
from jax.experimental import pallas as pl
from jax.experimental.pallas import tpu as pltpu
from jax.sharding import Mesh, PartitionSpec as P

BR = 128
FRONT = ("x", "z", "core")
ALL = ("x", "z", "core", "chain")
SLAB = ("x", "core", "chain")
LINE = ("x", "core")
SLOTS = 5
HOPS = 6
PEERS = 32
GROUPS = 8
LABEL_ROWS = 16
OWNED = 6
HOP_LANE = 64
STRAY_LANE = 125
COUNT_LANE = 126
OVER_LANE = 127
PIVOT_ROWS = 256
FLAG_ROWS = 8
UPDATE_ROWS = 512
SENT_ROWS = PIVOT_ROWS + 16


def slot_table(blocks, fronts, places, dest_count, slot_width):
    block_count = fronts.shape[0]
    sequence = jnp.arange(block_count, dtype=jnp.int32)
    earlier = (fronts[None, :] == fronts[:, None]) & (sequence[None, :] < sequence[:, None])
    rank_of = jnp.sum(earlier.astype(jnp.int32), axis=1)
    target = fronts * slot_width + rank_of
    source = jnp.full((dest_count * slot_width,), block_count, jnp.int32).at[target].set(sequence)
    slot_data = jnp.take(blocks, source, axis=0, mode="fill", fill_value=0)
    labels = jnp.take(places, source, axis=0, mode="fill", fill_value=-1)
    return (
        slot_data.reshape((dest_count, slot_width) + blocks.shape[1:]),
        labels.reshape(dest_count, slot_width),
    )


def full_exchange(child_blocks, fronts, places):
    slot_data, labels = slot_table(child_blocks, fronts, places, 128, 2)
    received = lax.all_to_all(slot_data, FRONT, split_axis=0, concat_axis=0, tiled=True)
    tags = lax.all_to_all(labels, FRONT, split_axis=0, concat_axis=0, tiled=True).reshape(-1)
    placed = jnp.where(
        tags < 8, tags // 2 * OWNED + tags % 2, (tags - 8) // 4 * OWNED + 2 + (tags - 8) % 4
    )
    placed = jnp.where(tags < 0, -1, placed)
    row_ids = jnp.arange(4 * OWNED, dtype=jnp.int32)
    onehot = (placed[None, :] == row_ids[:, None]).astype(jnp.bfloat16)
    flattened = received.reshape((-1,) + received.shape[2:])
    merged = jnp.einsum("km,mrs->krs", onehot, flattened, preferred_element_type=jnp.float32)
    return lax.psum_scatter(merged, "chain", scatter_dimension=0, tiled=True)


def write_tags(marks, tags, counts, strays, missed, count):
    lane = lax.broadcasted_iota(jnp.int32, (8, 128), 1)
    for peer in range(count):
        row = jnp.where(lane == COUNT_LANE, counts[peer].astype(jnp.float32), marks[peer])
        if strays is not None:
            row = jnp.where(lane == STRAY_LANE, strays[peer].astype(jnp.float32), row)
        row = jnp.where(lane == OVER_LANE, missed.astype(jnp.float32), row)
        tags[peer, 0:8, :] = row.astype(jnp.bfloat16)
        tags[peer, 8:16, :] = row.astype(jnp.bfloat16)


def send_kernel(spot, front, place, blocks, out, marks, tags, counts, strays, late, sem, tag_sem):
    for peer in range(PEERS):
        counts[peer] = 0
        strays[peer] = 0
    marks[...] = jnp.full(marks.shape, -1.0, jnp.float32)
    lane = lax.broadcasted_iota(jnp.int32, (8, 128), 1)

    def route(i):
        where_front = front[i]
        target = place[i]
        pivot = target < 8
        owner = jnp.where(pivot, target >> 1, (target - 8) >> 2)
        peer = ((where_front >> 5) * 2 + (where_front & 1)) * 4 + owner
        index = ((where_front >> 1) & 15) * OWNED + jnp.where(
            pivot, target & 1, 2 + ((target - 8) & 3)
        )
        live = target >= 0
        return live, jnp.where(live, peer, 0), index

    def launch(i, peer, used):
        pltpu.make_async_copy(
            blocks.at[i], out.at[peer, pl.ds(pl.multiple_of(used * BR, BR), BR)], sem
        ).start()

    def direct(i, carry):
        left, sent = carry
        live, peer, index = route(i)
        used = counts[peer]
        fits = live & (used < SLOTS)

        @pl.when(fits)
        def _():
            counts[peer] = used + 1
            launch(i, peer, used)
            marks[peer] = jnp.where(lane == used, index.astype(jnp.float32), marks[peer])

        @pl.when(live & (used >= SLOTS))
        def _():
            late[left] = i

        return (
            left + jnp.where(live & (used >= SLOTS), 1, 0),
            sent + jnp.where(fits, 1, 0),
        )

    left, sent = lax.fori_loop(0, front.shape[0], direct, (jnp.int32(0), jnp.int32(0)))

    def detour(k, carry):
        missed, sent = carry
        i = late[k]
        _, home, index = route(i)
        group = home >> 2
        chosen = jnp.int32(-1)
        for h in reversed(range(GROUPS - 1)):
            turn = lax.rem(spot[0] + k + h, GROUPS - 1)
            peer = (((group + 1 + turn) & 7) << 2) + (home & 3)
            chosen = jnp.where(counts[peer] < SLOTS, peer, chosen)
        fits = chosen >= 0

        @pl.when(fits)
        def _():
            used = counts[chosen]
            counts[chosen] = used + 1
            strays[chosen] = strays[chosen] + 1
            launch(i, chosen, used)
            row = jnp.where(lane == used, index.astype(jnp.float32), marks[chosen])
            marks[chosen] = jnp.where(lane == HOP_LANE + used, group.astype(jnp.float32), row)

        return missed + jnp.where(fits, 0, 1), sent + jnp.where(fits, 1, 0)

    missed, sent = lax.fori_loop(0, left, detour, (jnp.int32(0), sent))
    write_tags(marks, tags, counts, strays, missed, PEERS)
    tag_copy = pltpu.make_async_copy(tags, out.at[:, pl.ds(SLOTS * BR, LABEL_ROWS)], tag_sem)
    tag_copy.start()

    def drain(i, carry):
        pltpu.make_async_copy(blocks.at[0], out.at[0, pl.ds(0, BR)], sem).wait()
        return carry

    lax.fori_loop(0, sent, drain, 0)
    tag_copy.wait()


def pack(turn, fronts, places, blocks):
    smem = pl.BlockSpec(memory_space=pltpu.SMEM)
    return pl.pallas_call(
        send_kernel,
        out_shape=jax.ShapeDtypeStruct((PEERS, SLOTS * BR + LABEL_ROWS, 128), jnp.bfloat16),
        in_specs=[smem, smem, smem, pl.BlockSpec(memory_space=pltpu.VMEM)],
        out_specs=pl.BlockSpec(memory_space=pltpu.HBM),
        scratch_shapes=[
            pltpu.VMEM((PEERS, 8, 128), jnp.float32),
            pltpu.VMEM((PEERS, LABEL_ROWS, 128), jnp.bfloat16),
            pltpu.SMEM((PEERS,), jnp.int32),
            pltpu.SMEM((PEERS,), jnp.int32),
            pltpu.SMEM((128,), jnp.int32),
            pltpu.SemaphoreType.DMA,
            pltpu.SemaphoreType.DMA,
        ],
        name="pack",
    )(turn, fronts, places, blocks)


def forward_kernel(index, received, out, marks, tags, counts, sem, tag_sem):
    for peer in range(GROUPS):
        counts[peer] = 0
    marks[...] = jnp.full(marks.shape, -1.0, jnp.float32)
    lane = lax.broadcasted_iota(jnp.int32, (8, 128), 1)

    def source(i, carry):
        def slot(j, carry):
            missed, sent = carry
            home = index[i, 0, HOP_LANE + j]
            stray = home >= 0
            used = counts[jnp.maximum(home, 0)]
            fits = stray & (used < HOPS)

            @pl.when(fits)
            def _():
                counts[home] = used + 1
                pltpu.make_async_copy(
                    received.at[i, pl.ds(pl.multiple_of(j * BR, BR), BR)],
                    out.at[home, pl.ds(pl.multiple_of(used * BR, BR), BR)],
                    sem,
                ).start()
                target = index[i, 0, j].astype(jnp.float32)
                marks[home] = jnp.where(lane == used, target, marks[home])

            return (
                missed + jnp.where(stray & (used >= HOPS), 1, 0),
                sent + jnp.where(fits, 1, 0),
            )

        count = jnp.where(index[i, 0, STRAY_LANE] > 0, index[i, 0, COUNT_LANE], 0)
        return lax.fori_loop(0, count, slot, carry)

    missed, sent = lax.fori_loop(0, PEERS, source, (jnp.int32(0), jnp.int32(0)))
    write_tags(marks, tags, counts, None, missed, GROUPS)
    tag_copy = pltpu.make_async_copy(tags, out.at[:, pl.ds(HOPS * BR, LABEL_ROWS)], tag_sem)
    tag_copy.start()

    def drain(i, carry):
        pltpu.make_async_copy(received.at[0, pl.ds(0, BR)], out.at[0, pl.ds(0, BR)], sem).wait()
        return carry

    lax.fori_loop(0, sent, drain, 0)
    tag_copy.wait()


def forward(index, received):
    return pl.pallas_call(
        forward_kernel,
        out_shape=jax.ShapeDtypeStruct((GROUPS, HOPS * BR + LABEL_ROWS, 128), jnp.bfloat16),
        in_specs=[
            pl.BlockSpec(memory_space=pltpu.SMEM),
            pl.BlockSpec(memory_space=pl.ANY),
        ],
        out_specs=pl.BlockSpec(memory_space=pl.ANY),
        scratch_shapes=[
            pltpu.VMEM((GROUPS, 8, 128), jnp.float32),
            pltpu.VMEM((GROUPS, LABEL_ROWS, 128), jnp.bfloat16),
            pltpu.SMEM((GROUPS,), jnp.int32),
            pltpu.SemaphoreType.DMA,
            pltpu.SemaphoreType.DMA,
        ],
        compiler_params=pltpu.CompilerParams(vmem_limit_bytes=2 << 20),
        name="forward",
    )(index, received)


def gather_kernel(
    index, late_index, received, late, pivot_out, update_out, total, rounded, landed, sems, sem
):
    def fetch_from(array, labels, first):
        def fetch(i, at):
            def slot(j, spot):
                pltpu.make_async_copy(
                    array.at[i, pl.ds(pl.multiple_of(j * BR, BR), BR)],
                    landed.at[spot],
                    sems.at[first + i],
                ).start()
                return spot + 1

            return lax.fori_loop(0, labels[i, 0, COUNT_LANE], slot, at)

        return fetch

    def add_from(array, labels, first):
        def source(i, carry):
            missed, at = carry
            count = labels[i, 0, COUNT_LANE]

            def arrive(j, carry):
                pltpu.make_async_copy(
                    array.at[0, pl.ds(0, BR)], landed.at[0], sems.at[first + i]
                ).wait()
                return carry

            lax.fori_loop(0, count, arrive, 0)

            def slot(j, spot):
                target = labels[i, 0, j]
                chunk = target // OWNED
                start = pl.multiple_of((target - chunk * OWNED) * BR, BR)
                chunk = jnp.where(labels[i, 0, HOP_LANE + j] >= 0, 16, chunk)
                total[chunk, pl.ds(start, BR), :] += landed[spot].astype(jnp.float32)
                return spot + 1

            at = lax.fori_loop(0, count, slot, at)
            return missed + labels[i, 0, OVER_LANE], at

        return source

    at = lax.fori_loop(0, PEERS, fetch_from(received, index, 0), jnp.int32(0))
    lax.fori_loop(0, GROUPS, fetch_from(late, late_index, PEERS), at)
    total[0:16] = jnp.zeros((16, OWNED * BR, 128), jnp.float32)
    carry = (jnp.int32(0), jnp.int32(0))
    carry = lax.fori_loop(0, PEERS, add_from(received, index, 0), carry)
    missed, _ = lax.fori_loop(0, GROUPS, add_from(late, late_index, PEERS), carry)
    updates = pltpu.make_async_copy(
        total.at[pl.ds(0, 16), pl.ds(PIVOT_ROWS, UPDATE_ROWS)], update_out, sem
    )
    updates.start()
    rounded[:, 0:PIVOT_ROWS, :] = total[0:16, 0:PIVOT_ROWS, :].astype(jnp.bfloat16)
    rounded[:, PIVOT_ROWS:, :] = jnp.full((16, 16, 128), missed.astype(jnp.float32)).astype(
        jnp.bfloat16
    )
    pivots = pltpu.make_async_copy(rounded, pivot_out, sems.at[0])
    pivots.start()
    updates.wait()
    pivots.wait()


def add_up(index, late_index, received, late):
    smem = pl.BlockSpec(memory_space=pltpu.SMEM)
    anywhere = pl.BlockSpec(memory_space=pl.ANY)
    return pl.pallas_call(
        gather_kernel,
        out_shape=(
            jax.ShapeDtypeStruct((16, SENT_ROWS, 128), jnp.bfloat16),
            jax.ShapeDtypeStruct((16, UPDATE_ROWS, 128), jnp.float32),
        ),
        in_specs=[smem, smem, anywhere, anywhere],
        out_specs=(anywhere, pl.BlockSpec(memory_space=pltpu.HBM)),
        scratch_shapes=[
            pltpu.VMEM((17, OWNED * BR, 128), jnp.float32),
            pltpu.VMEM((16, SENT_ROWS, 128), jnp.bfloat16),
            pltpu.VMEM((PEERS * SLOTS + GROUPS * HOPS, BR, 128), jnp.bfloat16),
            pltpu.SemaphoreType.DMA((PEERS + GROUPS,)),
            pltpu.SemaphoreType.DMA,
        ],
        name="add_up",
    )(index, late_index, received, late)


def solve_kernel(spot, pivots, rhs, lower, inverse, update, solved_out, product_out, kept):
    chain_at = spot[0]
    live_count = pivots[0]
    for block in range(4):
        rows = slice(block * PIVOT_ROWS, (block + 1) * PIVOT_ROWS)
        at = block * (PIVOT_ROWS + FLAG_ROWS)
        partial = rhs[at : at + PIVOT_ROWS, :]
        if block > 0:
            partial = partial - jnp.dot(
                lower[rows, 0 : block * PIVOT_ROWS],
                kept[0 : block * PIVOT_ROWS, :],
                preferred_element_type=jnp.float32,
            )
        row = block * PIVOT_ROWS + lax.broadcasted_iota(jnp.int32, (PIVOT_ROWS, 128), 0)
        product = jnp.dot(
            inverse[rows, :],
            partial,
            precision=lax.Precision.HIGHEST,
            preferred_element_type=jnp.float32,
        )
        here = jnp.where(row < live_count, product, 0.0)
        kept[rows, :] = here.astype(jnp.bfloat16)

        @pl.when(chain_at == block)
        def _():
            solved_out[...] = here

    product_out[...] = jnp.dot(update[...], kept[...], preferred_element_type=jnp.float32)


def solve(spot, pivots, rhs, lower, inverse, update):
    smem = pl.BlockSpec(memory_space=pltpu.SMEM)
    vmem = pl.BlockSpec(memory_space=pltpu.VMEM)
    return pl.pallas_call(
        solve_kernel,
        out_shape=(
            jax.ShapeDtypeStruct((PIVOT_ROWS, 128), jnp.float32),
            jax.ShapeDtypeStruct((UPDATE_ROWS, 128), jnp.float32),
        ),
        in_specs=[smem, smem] + [vmem] * 4,
        out_specs=(vmem, vmem),
        scratch_shapes=[pltpu.VMEM((4 * PIVOT_ROWS, 128), jnp.bfloat16)],
        compiler_params=pltpu.CompilerParams(vmem_limit_bytes=16 << 20),
        name="solve",
    )(spot, pivots, rhs, lower, inverse, update)


def labels_of(received):
    return received[:, -LABEL_ROWS : 1 - LABEL_ROWS, :].astype(jnp.int32)


def body(
    rhs, child_blocks, dest_front, dest_place, front_pivots, diag_inv, lower_factor, update_factor
):
    fronts = dest_front.reshape(-1)
    spot = lax.axis_index("chain").astype(jnp.int32).reshape(1)
    turn = lax.axis_index(LINE).astype(jnp.int32).reshape(1) + 2 * spot
    lower = lax.all_gather(lower_factor, "chain", axis=0, tiled=True)
    inverse = lax.all_gather(diag_inv, "chain", axis=0, tiled=True)
    packed = pack(turn, fronts, dest_place, child_blocks)
    received = lax.all_to_all(packed, SLAB, split_axis=0, concat_axis=0, tiled=True)
    received, lower, inverse = lax.optimization_barrier((received, lower, inverse))
    index = labels_of(received)
    late = lax.all_to_all(forward(index, received), LINE, split_axis=0, concat_axis=0, tiled=True)
    pivot_sums, update_sums = add_up(index, labels_of(late), received, late)
    update_start = lax.psum_scatter(update_sums, "z", scatter_dimension=0, tiled=True)
    update_start = lax.optimization_barrier(update_start).reshape(UPDATE_ROWS, 128)
    pivot_parts = lax.all_to_all(pivot_sums, "z", split_axis=0, concat_axis=0, tiled=True)
    parts = pivot_parts[:, : PIVOT_ROWS + FLAG_ROWS].astype(jnp.float32)
    padded = jnp.pad(rhs, ((0, FLAG_ROWS), (0, 0)))

    def share(mine):
        return lax.all_gather(padded + mine, "chain", axis=0, tiled=True)

    def general(solved, product, start):
        blocks = full_exchange(child_blocks, fronts, dest_place).reshape(OWNED * BR, 128)
        mine = jnp.pad(blocks[:PIVOT_ROWS], ((0, FLAG_ROWS), (0, 0)))
        solved, product = solve(spot, front_pivots, share(mine), lower, inverse, update_factor)
        return solved, blocks[PIVOT_ROWS:] - product

    def finish(solved, product, start):
        return solved, start - product

    all_rhs = share(jnp.sum(parts, axis=0))
    missed = jnp.sum(all_rhs.reshape(4, PIVOT_ROWS + FLAG_ROWS, 128)[:, PIVOT_ROWS, 0])
    solved, product = solve(spot, front_pivots, all_rhs, lower, inverse, update_factor)
    return lax.cond(missed > 0, general, finish, solved, product, update_start)


def solution(mesh):
    grid = Mesh(mesh.devices.reshape(4, 16, 2, 4), ALL)
    rows = P(ALL, None)
    return jax.shard_map(
        body,
        mesh=grid,
        in_specs=(rows, P(ALL, None, None), rows, P(ALL), P(FRONT), rows, rows, rows),
        out_specs=(rows, rows),
        check_vma=False,
    )
```

```python
import jax
import jax.numpy as jnp
from jax import lax
from jax.experimental import pallas as pl
from jax.experimental.pallas import tpu as pltpu
from jax.sharding import Mesh, PartitionSpec as P

BR = 128
FRONT = ("x", "z", "core")
ALL = ("x", "z", "core", "chain")
SLAB = ("x", "core", "chain")
LINE = ("x", "core")
SLOTS = 5
HOPS = 6
PEERS = 32
GROUPS = 8
LABEL_ROWS = 16
OWNED = 6
HOP_LANE = 64
STRAY_LANE = 125
COUNT_LANE = 126
OVER_LANE = 127
PIVOT_ROWS = 256
FLAG_ROWS = 8
CHUNK = OWNED * BR + FLAG_ROWS


def slot_table(blocks, fronts, places, dest_count, slot_width):
    block_count = fronts.shape[0]
    sequence = jnp.arange(block_count, dtype=jnp.int32)
    earlier = (fronts[None, :] == fronts[:, None]) & (sequence[None, :] < sequence[:, None])
    rank_of = jnp.sum(earlier.astype(jnp.int32), axis=1)
    target = fronts * slot_width + rank_of
    source = jnp.full((dest_count * slot_width,), block_count, jnp.int32).at[target].set(sequence)
    slot_data = jnp.take(blocks, source, axis=0, mode="fill", fill_value=0)
    labels = jnp.take(places, source, axis=0, mode="fill", fill_value=-1)
    return (
        slot_data.reshape((dest_count, slot_width) + blocks.shape[1:]),
        labels.reshape(dest_count, slot_width),
    )


def full_exchange(child_blocks, fronts, places):
    slot_data, labels = slot_table(child_blocks, fronts, places, 128, 2)
    received = lax.all_to_all(slot_data, FRONT, split_axis=0, concat_axis=0, tiled=True)
    tags = lax.all_to_all(labels, FRONT, split_axis=0, concat_axis=0, tiled=True).reshape(-1)
    placed = jnp.where(
        tags < 8, tags // 2 * OWNED + tags % 2, (tags - 8) // 4 * OWNED + 2 + (tags - 8) % 4
    )
    placed = jnp.where(tags < 0, -1, placed)
    row_ids = jnp.arange(4 * OWNED, dtype=jnp.int32)
    onehot = (placed[None, :] == row_ids[:, None]).astype(jnp.bfloat16)
    flattened = received.reshape((-1,) + received.shape[2:])
    merged = jnp.einsum("km,mrs->krs", onehot, flattened, preferred_element_type=jnp.float32)
    return lax.psum_scatter(merged, "chain", scatter_dimension=0, tiled=True)


def write_tags(marks, tags, counts, strays, missed, count):
    lane = lax.broadcasted_iota(jnp.int32, (8, 128), 1)
    for peer in range(count):
        row = jnp.where(lane == COUNT_LANE, counts[peer].astype(jnp.float32), marks[peer])
        if strays is not None:
            row = jnp.where(lane == STRAY_LANE, strays[peer].astype(jnp.float32), row)
        row = jnp.where(lane == OVER_LANE, missed.astype(jnp.float32), row)
        tags[peer, 0:8, :] = row.astype(jnp.bfloat16)
        tags[peer, 8:16, :] = row.astype(jnp.bfloat16)


def send_kernel(spot, front, place, blocks, out, marks, tags, counts, strays, late, sem, tag_sem):
    for peer in range(PEERS):
        counts[peer] = 0
        strays[peer] = 0
    marks[...] = jnp.full(marks.shape, -1.0, jnp.float32)
    lane = lax.broadcasted_iota(jnp.int32, (8, 128), 1)

    def route(i):
        where_front = front[i]
        target = place[i]
        pivot = target < 8
        owner = jnp.where(pivot, target >> 1, (target - 8) >> 2)
        peer = ((where_front >> 5) * 2 + (where_front & 1)) * 4 + owner
        index = ((where_front >> 1) & 15) * OWNED + jnp.where(
            pivot, target & 1, 2 + ((target - 8) & 3)
        )
        live = target >= 0
        return live, jnp.where(live, peer, 0), index

    def launch(i, peer, used):
        pltpu.make_async_copy(
            blocks.at[i], out.at[peer, pl.ds(pl.multiple_of(used * BR, BR), BR)], sem
        ).start()

    def direct(i, carry):
        left, sent = carry
        live, peer, index = route(i)
        used = counts[peer]
        fits = live & (used < SLOTS)

        @pl.when(fits)
        def _():
            counts[peer] = used + 1
            launch(i, peer, used)
            marks[peer] = jnp.where(lane == used, index.astype(jnp.float32), marks[peer])

        @pl.when(live & (used >= SLOTS))
        def _():
            late[left] = i

        return (
            left + jnp.where(live & (used >= SLOTS), 1, 0),
            sent + jnp.where(fits, 1, 0),
        )

    left, sent = lax.fori_loop(0, front.shape[0], direct, (jnp.int32(0), jnp.int32(0)))

    def detour(k, carry):
        missed, sent = carry
        i = late[k]
        _, home, index = route(i)
        group = home >> 2
        chosen = jnp.int32(-1)
        for h in reversed(range(GROUPS - 1)):
            turn = lax.rem(spot[0] + k + h, GROUPS - 1)
            peer = (((group + 1 + turn) & 7) << 2) + (home & 3)
            chosen = jnp.where(counts[peer] < SLOTS, peer, chosen)
        fits = chosen >= 0

        @pl.when(fits)
        def _():
            used = counts[chosen]
            counts[chosen] = used + 1
            strays[chosen] = strays[chosen] + 1
            launch(i, chosen, used)
            row = jnp.where(lane == used, index.astype(jnp.float32), marks[chosen])
            marks[chosen] = jnp.where(lane == HOP_LANE + used, group.astype(jnp.float32), row)

        return missed + jnp.where(fits, 0, 1), sent + jnp.where(fits, 1, 0)

    missed, sent = lax.fori_loop(0, left, detour, (jnp.int32(0), sent))
    write_tags(marks, tags, counts, strays, missed, PEERS)
    tag_copy = pltpu.make_async_copy(tags, out.at[:, pl.ds(SLOTS * BR, LABEL_ROWS)], tag_sem)
    tag_copy.start()

    def drain(i, carry):
        pltpu.make_async_copy(blocks.at[0], out.at[0, pl.ds(0, BR)], sem).wait()
        return carry

    lax.fori_loop(0, sent, drain, 0)
    tag_copy.wait()


def pack(turn, fronts, places, blocks):
    smem = pl.BlockSpec(memory_space=pltpu.SMEM)
    return pl.pallas_call(
        send_kernel,
        out_shape=jax.ShapeDtypeStruct((PEERS, SLOTS * BR + LABEL_ROWS, 128), jnp.bfloat16),
        in_specs=[smem, smem, smem, pl.BlockSpec(memory_space=pltpu.VMEM)],
        out_specs=pl.BlockSpec(memory_space=pl.ANY),
        scratch_shapes=[
            pltpu.VMEM((PEERS, 8, 128), jnp.float32),
            pltpu.VMEM((PEERS, LABEL_ROWS, 128), jnp.bfloat16),
            pltpu.SMEM((PEERS,), jnp.int32),
            pltpu.SMEM((PEERS,), jnp.int32),
            pltpu.SMEM((128,), jnp.int32),
            pltpu.SemaphoreType.DMA,
            pltpu.SemaphoreType.DMA,
        ],
        name="pack",
    )(turn, fronts, places, blocks)


def forward_kernel(index, received, out, marks, tags, counts, staged, homes, rows, sem, tag_sem):
    for peer in range(GROUPS):
        counts[peer] = 0
    marks[...] = jnp.full(marks.shape, -1.0, jnp.float32)
    lane = lax.broadcasted_iota(jnp.int32, (8, 128), 1)

    def source(i, carry):
        def slot(j, carry):
            missed, sent = carry
            home = index[i, 0, HOP_LANE + j]
            stray = home >= 0
            used = counts[jnp.maximum(home, 0)]
            fits = stray & (used < HOPS)

            @pl.when(fits)
            def _():
                counts[home] = used + 1
                homes[sent] = home
                rows[sent] = used * BR
                pltpu.make_async_copy(
                    received.at[i, pl.ds(pl.multiple_of(j * BR, BR), BR)], staged.at[sent], sem
                ).start()
                target = index[i, 0, j].astype(jnp.float32)
                marks[home] = jnp.where(lane == used, target, marks[home])

            return (
                missed + jnp.where(stray & (used >= HOPS), 1, 0),
                sent + jnp.where(fits, 1, 0),
            )

        count = jnp.where(index[i, 0, STRAY_LANE] > 0, index[i, 0, COUNT_LANE], 0)
        return lax.fori_loop(0, count, slot, carry)

    missed, sent = lax.fori_loop(0, PEERS, source, (jnp.int32(0), jnp.int32(0)))
    write_tags(marks, tags, counts, None, missed, GROUPS)
    tag_copy = pltpu.make_async_copy(tags, out.at[:, pl.ds(HOPS * BR, LABEL_ROWS)], tag_sem)
    tag_copy.start()

    def arrive(i, carry):
        pltpu.make_async_copy(received.at[0, pl.ds(0, BR)], staged.at[0], sem).wait()
        return carry

    def leave(k, carry):
        row = pl.multiple_of(rows[k], BR)
        pltpu.make_async_copy(staged.at[k], out.at[homes[k], pl.ds(row, BR)], sem).start()
        return carry

    def left(k, carry):
        pltpu.make_async_copy(staged.at[0], out.at[0, pl.ds(0, BR)], sem).wait()
        return carry

    lax.fori_loop(0, sent, arrive, 0)
    lax.fori_loop(0, sent, leave, 0)
    lax.fori_loop(0, sent, left, 0)
    tag_copy.wait()


def forward(index, received):
    return pl.pallas_call(
        forward_kernel,
        out_shape=jax.ShapeDtypeStruct((GROUPS, HOPS * BR + LABEL_ROWS, 128), jnp.bfloat16),
        in_specs=[
            pl.BlockSpec(memory_space=pltpu.SMEM),
            pl.BlockSpec(memory_space=pl.ANY),
        ],
        out_specs=pl.BlockSpec(memory_space=pl.ANY),
        scratch_shapes=[
            pltpu.VMEM((GROUPS, 8, 128), jnp.float32),
            pltpu.VMEM((GROUPS, LABEL_ROWS, 128), jnp.bfloat16),
            pltpu.SMEM((GROUPS,), jnp.int32),
            pltpu.VMEM((GROUPS * HOPS, BR, 128), jnp.bfloat16),
            pltpu.SMEM((GROUPS * HOPS,), jnp.int32),
            pltpu.SMEM((GROUPS * HOPS,), jnp.int32),
            pltpu.SemaphoreType.DMA,
            pltpu.SemaphoreType.DMA,
        ],
        name="forward",
    )(index, received)


def target_of(target):
    chunk = target // OWNED
    row = target - chunk * OWNED
    return chunk, pl.multiple_of(row * BR + jnp.where(row >= 2, FLAG_ROWS, 0), 8)


def direct_kernel(index, received, out, total, landed, sems, sem):
    def fetch(i, at):
        def slot(j, spot):
            pltpu.make_async_copy(
                received.at[i, pl.ds(pl.multiple_of(j * BR, BR), BR)], landed.at[spot], sems.at[i]
            ).start()
            return spot + 1

        return lax.fori_loop(0, index[i, 0, COUNT_LANE], slot, at)

    lax.fori_loop(0, PEERS, fetch, jnp.int32(0))
    total[0:16] = jnp.zeros((16, CHUNK, 128), jnp.float32)

    def source(i, carry):
        missed, at = carry
        count = index[i, 0, COUNT_LANE]

        def arrive(j, carry):
            pltpu.make_async_copy(received.at[0, pl.ds(0, BR)], landed.at[0], sems.at[i]).wait()
            return carry

        lax.fori_loop(0, count, arrive, 0)

        def slot(j, spot):
            chunk, start = target_of(index[i, 0, j])
            chunk = jnp.where(index[i, 0, HOP_LANE + j] >= 0, 16, chunk)
            total[chunk, pl.ds(start, BR), :] += landed[spot].astype(jnp.float32)
            return spot + 1

        at = lax.fori_loop(0, count, slot, at)
        return missed + index[i, 0, OVER_LANE], at

    missed, _ = lax.fori_loop(0, PEERS, source, (jnp.int32(0), jnp.int32(0)))
    total[0:16, PIVOT_ROWS : PIVOT_ROWS + FLAG_ROWS, :] = jnp.full(
        (16, FLAG_ROWS, 128), missed.astype(jnp.float32)
    )
    copy = pltpu.make_async_copy(total.at[pl.ds(0, 16)], out, sem)
    copy.start()
    copy.wait()


def add_direct(index, received):
    return pl.pallas_call(
        direct_kernel,
        out_shape=jax.ShapeDtypeStruct((16, CHUNK, 128), jnp.float32),
        in_specs=[
            pl.BlockSpec(memory_space=pltpu.SMEM),
            pl.BlockSpec(memory_space=pl.ANY),
        ],
        out_specs=pl.BlockSpec(memory_space=pltpu.HBM),
        scratch_shapes=[
            pltpu.VMEM((17, CHUNK, 128), jnp.float32),
            pltpu.VMEM((PEERS * SLOTS, BR, 128), jnp.bfloat16),
            pltpu.SemaphoreType.DMA((PEERS,)),
            pltpu.SemaphoreType.DMA,
        ],
        name="add_direct",
    )(index, received)


def late_kernel(labels, late, dense, out, blocks, sums, flags, targets, homes, sem, sum_sem):
    def fetch(i, carry):
        def slot(j, carry):
            at, kept = carry
            target = labels[i, 0, j]

            def match(k, found):
                return jnp.where(targets[k] == target, k, found)

            found = lax.fori_loop(0, kept, match, jnp.int32(-1))
            fresh = found < 0
            homes[at] = jnp.where(fresh, kept, found)
            pltpu.make_async_copy(
                late.at[i, pl.ds(pl.multiple_of(j * BR, BR), BR)], blocks.at[at], sem
            ).start()

            @pl.when(fresh)
            def _():
                targets[kept] = target
                chunk, start = target_of(target)
                pltpu.make_async_copy(
                    dense.at[chunk, pl.ds(start, BR)], sums.at[kept], sum_sem
                ).start()

            return at + 1, kept + jnp.where(fresh, 1, 0)

        at, kept, missed = carry
        at, kept = lax.fori_loop(0, labels[i, 0, COUNT_LANE], slot, (at, kept))
        return at, kept, missed + labels[i, 0, OVER_LANE]

    zero = jnp.int32(0)
    count, kept, missed = lax.fori_loop(0, GROUPS, fetch, (zero, zero, zero))

    def arrive_block(k, carry):
        pltpu.make_async_copy(late.at[0, pl.ds(0, BR)], blocks.at[0], sem).wait()
        return carry

    def arrive_sum(k, carry):
        pltpu.make_async_copy(dense.at[0, pl.ds(0, BR)], sums.at[0], sum_sem).wait()
        return carry

    lax.fori_loop(0, count, arrive_block, 0)
    lax.fori_loop(0, kept, arrive_sum, 0)

    def add(k, carry):
        sums[homes[k]] += blocks[k].astype(jnp.float32)
        return carry

    lax.fori_loop(0, count, add, 0)

    def leave(k, carry):
        chunk, start = target_of(targets[k])
        pltpu.make_async_copy(sums.at[k], out.at[chunk, pl.ds(start, BR)], sum_sem).start()
        return carry

    def left(k, carry):
        pltpu.make_async_copy(sums.at[0], out.at[0, pl.ds(0, BR)], sum_sem).wait()
        return carry

    lax.fori_loop(0, kept, leave, 0)

    @pl.when(missed > 0)
    def _():
        flags[...] = jnp.full(flags.shape, missed.astype(jnp.float32))
        mark = pltpu.make_async_copy(flags, out.at[:, pl.ds(PIVOT_ROWS, FLAG_ROWS)], sem)
        mark.start()
        mark.wait()

    lax.fori_loop(0, kept, left, 0)


def add_late(labels, late, dense):
    most = GROUPS * HOPS
    anywhere = pl.BlockSpec(memory_space=pl.ANY)
    in_hbm = pl.BlockSpec(memory_space=pltpu.HBM)
    return pl.pallas_call(
        late_kernel,
        out_shape=jax.ShapeDtypeStruct((16, CHUNK, 128), jnp.float32),
        in_specs=[pl.BlockSpec(memory_space=pltpu.SMEM), anywhere, in_hbm],
        out_specs=in_hbm,
        input_output_aliases={2: 0},
        scratch_shapes=[
            pltpu.VMEM((most, BR, 128), jnp.bfloat16),
            pltpu.VMEM((most, BR, 128), jnp.float32),
            pltpu.VMEM((16, FLAG_ROWS, 128), jnp.float32),
            pltpu.SMEM((most,), jnp.int32),
            pltpu.SMEM((most,), jnp.int32),
            pltpu.SemaphoreType.DMA,
            pltpu.SemaphoreType.DMA,
        ],
        name="add_late",
    )(labels, late, dense)


def solve_kernel(spot, pivots, rhs, *refs):
    lowers, inverses = refs[0:4], refs[4:8]
    update, solved_out, product_out, lower, inverse, kept = refs[8:]
    chain_at = spot[0]
    live_count = pivots[0]
    for shift in range(4):
        block = (chain_at - shift) & 3
        lower[block] = lowers[shift][...]
        inverse[block] = inverses[shift][...]
    for block in range(4):
        rows = slice(block * 256, (block + 1) * 256)
        at = block * (PIVOT_ROWS + FLAG_ROWS)
        partial = rhs[at : at + PIVOT_ROWS, :]
        if block > 0:
            partial = partial - jnp.dot(
                lower[block, :, 0 : block * 256],
                kept[0 : block * 256, :],
                preferred_element_type=jnp.float32,
            )
        row = block * 256 + lax.broadcasted_iota(jnp.int32, (256, 128), 0)
        product = jnp.dot(
            inverse[block],
            partial,
            precision=lax.Precision.HIGHEST,
            preferred_element_type=jnp.float32,
        )
        here = jnp.where(row < live_count, product, 0.0)
        kept[rows, :] = here.astype(jnp.bfloat16)

        @pl.when(chain_at == block)
        def _():
            solved_out[...] = here

    product_out[...] = jnp.dot(update[...], kept[...], preferred_element_type=jnp.float32)


def solve(spot, pivots, rhs, lowers, inverses, update):
    smem = pl.BlockSpec(memory_space=pltpu.SMEM)
    vmem = pl.BlockSpec(memory_space=pltpu.VMEM)
    return pl.pallas_call(
        solve_kernel,
        out_shape=(
            jax.ShapeDtypeStruct((256, 128), jnp.float32),
            jax.ShapeDtypeStruct((512, 128), jnp.float32),
        ),
        in_specs=[smem, smem] + [vmem] * 10,
        out_specs=(vmem, vmem),
        scratch_shapes=[
            pltpu.VMEM((4, 256, 768), jnp.bfloat16),
            pltpu.VMEM((4, 256, 256), jnp.float32),
            pltpu.VMEM((1024, 128), jnp.bfloat16),
        ],
        compiler_params=pltpu.CompilerParams(vmem_limit_bytes=20 << 20),
        name="solve",
    )(spot, pivots, rhs, *lowers, *inverses, update)


def around_chain(value):
    moved = [
        lax.ppermute(value, "chain", [(i, (i + shift) % 4) for i in range(4)])
        for shift in (1, 2, 3)
    ]
    return (value, *moved)


def labels_of(received):
    return received[:, -LABEL_ROWS : 1 - LABEL_ROWS, :].astype(jnp.int32)


def body(
    rhs, child_blocks, dest_front, dest_place, front_pivots, diag_inv, lower_factor, update_factor
):
    fronts = dest_front.reshape(-1)
    spot = lax.axis_index("chain").astype(jnp.int32).reshape(1)
    turn = lax.axis_index(LINE).astype(jnp.int32).reshape(1) + 2 * spot
    packed = pack(turn, fronts, dest_place, child_blocks)
    received = lax.all_to_all(packed, SLAB, split_axis=0, concat_axis=0, tiled=True)
    index = labels_of(received)
    late = lax.all_to_all(forward(index, received), LINE, split_axis=0, concat_axis=0, tiled=True)
    dense = add_late(labels_of(late), late, add_direct(index, received))
    dense, lower_factor, diag_inv = lax.optimization_barrier((dense, lower_factor, diag_inv))
    owned = lax.psum_scatter(dense, "z", scatter_dimension=0, tiled=True)
    lowers = around_chain(lower_factor)
    inverses = around_chain(diag_inv)
    owned, lowers, inverses = lax.optimization_barrier((owned, lowers, inverses))
    owned = owned.reshape(CHUNK, 128)

    def share(mine):
        padded = jnp.pad(rhs, ((0, FLAG_ROWS), (0, 0)))
        return lax.all_gather(
            padded + mine[: PIVOT_ROWS + FLAG_ROWS], "chain", axis=0, tiled=True
        )

    def outputs(all_rhs, mine, lowers, inverses):
        solved, product = solve(spot, front_pivots, all_rhs, lowers, inverses, update_factor)
        return solved, mine[PIVOT_ROWS + FLAG_ROWS :] - product

    def general(solved, updated):
        blocks = full_exchange(child_blocks, fronts, dest_place).reshape(OWNED * BR, 128)
        flags = jnp.zeros((FLAG_ROWS, 128), jnp.float32)
        mine = jnp.concatenate([blocks[:PIVOT_ROWS], flags, blocks[PIVOT_ROWS:]])
        factors = around_chain(lower_factor), around_chain(diag_inv)
        return outputs(share(mine), mine, *factors)

    all_rhs = share(owned)
    over = jnp.sum(all_rhs.reshape(4, PIVOT_ROWS + FLAG_ROWS, 128)[:, PIVOT_ROWS, 0])
    solved, updated = outputs(all_rhs, owned, lowers, inverses)
    return lax.cond(over > 0, general, lambda *fast: fast, solved, updated)


def solution(mesh):
    grid = Mesh(mesh.devices.reshape(4, 16, 2, 4), ALL)
    rows = P(ALL, None)
    return jax.shard_map(
        body,
        mesh=grid,
        in_specs=(rows, P(ALL, None, None), rows, P(ALL), P(FRONT), rows, rows, rows),
        out_specs=(rows, rows),
        check_vma=False,
    )
```

```python
import jax
import jax.numpy as jnp
from jax import lax
from jax.experimental import pallas as pl
from jax.experimental.pallas import tpu as pltpu
from jax.sharding import Mesh, PartitionSpec as P

BR = 128
FRONT = ("x", "z", "core")
ALL = ("x", "z", "core", "chain")
SLAB = ("x", "core", "chain")
LINE = ("x", "core")
SLOTS = 5
HOPS = 5
PEERS = 32
GROUPS = 8
LABEL_ROWS = 16
OWNED = 6
HOP_LANE = 64
STRAY_LANE = 125
COUNT_LANE = 126
OVER_LANE = 127
PIVOT_ROWS = 256
FLAG_ROWS = 8
CHUNK = OWNED * BR + FLAG_ROWS


def slot_table(blocks, fronts, places, dest_count, slot_width):
    block_count = fronts.shape[0]
    sequence = jnp.arange(block_count, dtype=jnp.int32)
    earlier = (fronts[None, :] == fronts[:, None]) & (sequence[None, :] < sequence[:, None])
    rank_of = jnp.sum(earlier.astype(jnp.int32), axis=1)
    target = fronts * slot_width + rank_of
    source = jnp.full((dest_count * slot_width,), block_count, jnp.int32).at[target].set(sequence)
    slot_data = jnp.take(blocks, source, axis=0, mode="fill", fill_value=0)
    labels = jnp.take(places, source, axis=0, mode="fill", fill_value=-1)
    return (
        slot_data.reshape((dest_count, slot_width) + blocks.shape[1:]),
        labels.reshape(dest_count, slot_width),
    )


def full_exchange(child_blocks, fronts, places):
    slot_data, labels = slot_table(child_blocks, fronts, places, 128, 2)
    received = lax.all_to_all(slot_data, FRONT, split_axis=0, concat_axis=0, tiled=True)
    tags = lax.all_to_all(labels, FRONT, split_axis=0, concat_axis=0, tiled=True).reshape(-1)
    placed = jnp.where(
        tags < 8, tags // 2 * OWNED + tags % 2, (tags - 8) // 4 * OWNED + 2 + (tags - 8) % 4
    )
    placed = jnp.where(tags < 0, -1, placed)
    row_ids = jnp.arange(4 * OWNED, dtype=jnp.int32)
    onehot = (placed[None, :] == row_ids[:, None]).astype(jnp.bfloat16)
    flattened = received.reshape((-1,) + received.shape[2:])
    merged = jnp.einsum("km,mrs->krs", onehot, flattened, preferred_element_type=jnp.float32)
    return lax.psum_scatter(merged, "chain", scatter_dimension=0, tiled=True)


def write_tags(marks, tags, counts, strays, missed, count):
    lane = lax.broadcasted_iota(jnp.int32, (8, 128), 1)
    for peer in range(count):
        row = jnp.where(lane == COUNT_LANE, counts[peer].astype(jnp.float32), marks[peer])
        if strays is not None:
            row = jnp.where(lane == STRAY_LANE, strays[peer].astype(jnp.float32), row)
        row = jnp.where(lane == OVER_LANE, missed.astype(jnp.float32), row)
        tags[peer, 0:8, :] = row.astype(jnp.bfloat16)
        tags[peer, 8:16, :] = row.astype(jnp.bfloat16)


def send_kernel(
    spot, front, place, source, out, marks, tags, counts, strays, seen, late, slots, blocks, sem, tag_sem, in_sem
):
    load = pltpu.make_async_copy(source, blocks, in_sem)
    load.start()
    for peer in range(PEERS):
        counts[peer] = 0
        strays[peer] = 0
        seen[peer] = 0
    marks[...] = jnp.full(marks.shape, -1.0, jnp.float32)
    lane = lax.broadcasted_iota(jnp.int32, (8, 128), 1)

    def route(i):
        where_front = front[i]
        target = place[i]
        pivot = target < 8
        owner = jnp.where(pivot, target >> 1, (target - 8) >> 2)
        peer = ((where_front >> 5) * 2 + (where_front & 1)) * 4 + owner
        index = ((where_front >> 1) & 15) * OWNED + jnp.where(
            pivot, target & 1, 2 + ((target - 8) & 3)
        )
        live = target >= 0
        return live, jnp.where(live, peer, 0), index

    def launch(i, carry):
        peer = slots[i] >> 3
        used = slots[i] & 7

        @pl.when(slots[i] >= 0)
        def _():
            pltpu.make_async_copy(
                blocks.at[i], out.at[peer, pl.ds(pl.multiple_of(used * BR, BR), BR)], sem
            ).start()

        return carry

    def direct(i, carry):
        left, sent = carry
        live, peer, index = route(i)
        used = counts[peer]
        fits = live & (used < SLOTS)
        slots[i] = -1

        @pl.when(fits)
        def _():
            counts[peer] = used + 1
            slots[i] = (peer << 3) + used
            marks[peer] = jnp.where(lane == used, index.astype(jnp.float32), marks[peer])

        @pl.when(live & (used >= SLOTS))
        def _():
            late[left] = i

        return (
            left + jnp.where(live & (used >= SLOTS), 1, 0),
            sent + jnp.where(fits, 1, 0),
        )

    left, sent = lax.fori_loop(0, front.shape[0], direct, (jnp.int32(0), jnp.int32(0)))

    def detour(k, carry):
        missed, sent = carry
        i = late[k]
        _, home, index = route(i)
        group = home >> 2
        first = spot[0] + 3 * seen[home]
        seen[home] = seen[home] + 1
        chosen = jnp.int32(-1)
        for h in reversed(range(GROUPS - 1)):
            turn = lax.rem(first + h, GROUPS - 1)
            peer = (((group + 1 + turn) & 7) << 2) + (home & 3)
            chosen = jnp.where(counts[peer] < SLOTS, peer, chosen)
        fits = chosen >= 0

        @pl.when(fits)
        def _():
            used = counts[chosen]
            counts[chosen] = used + 1
            strays[chosen] = strays[chosen] + 1
            slots[i] = (chosen << 3) + used
            row = jnp.where(lane == used, index.astype(jnp.float32), marks[chosen])
            marks[chosen] = jnp.where(lane == HOP_LANE + used, group.astype(jnp.float32), row)

        return missed + jnp.where(fits, 0, 1), sent + jnp.where(fits, 1, 0)

    missed, sent = lax.fori_loop(0, left, detour, (jnp.int32(0), sent))
    load.wait()
    lax.fori_loop(0, front.shape[0], launch, 0)
    write_tags(marks, tags, counts, strays, missed, PEERS)
    tag_copy = pltpu.make_async_copy(tags, out.at[:, pl.ds(SLOTS * BR, LABEL_ROWS)], tag_sem)
    tag_copy.start()

    def drain(i, carry):
        pltpu.make_async_copy(blocks.at[0], out.at[0, pl.ds(0, BR)], sem).wait()
        return carry

    lax.fori_loop(0, sent, drain, 0)
    tag_copy.wait()


def pack(turn, fronts, places, blocks):
    smem = pl.BlockSpec(memory_space=pltpu.SMEM)
    return pl.pallas_call(
        send_kernel,
        out_shape=jax.ShapeDtypeStruct((PEERS, SLOTS * BR + LABEL_ROWS, 128), jnp.bfloat16),
        in_specs=[smem, smem, smem, pl.BlockSpec(memory_space=pl.ANY)],
        out_specs=pl.BlockSpec(memory_space=pl.ANY),
        scratch_shapes=[
            pltpu.VMEM((PEERS, 8, 128), jnp.float32),
            pltpu.VMEM((PEERS, LABEL_ROWS, 128), jnp.bfloat16),
            pltpu.SMEM((PEERS,), jnp.int32),
            pltpu.SMEM((PEERS,), jnp.int32),
            pltpu.SMEM((PEERS,), jnp.int32),
            pltpu.SMEM((128,), jnp.int32),
            pltpu.SMEM((128,), jnp.int32),
            pltpu.VMEM(blocks.shape, jnp.bfloat16),
            pltpu.SemaphoreType.DMA,
            pltpu.SemaphoreType.DMA,
            pltpu.SemaphoreType.DMA,
        ],
        name="pack",
    )(turn, fronts, places, blocks)


def forward_kernel(index, received, out, marks, tags, counts, staged, homes, rows, sem, tag_sem):
    for peer in range(GROUPS):
        counts[peer] = 0
    marks[...] = jnp.full(marks.shape, -1.0, jnp.float32)
    lane = lax.broadcasted_iota(jnp.int32, (8, 128), 1)

    def source(i, carry):
        def slot(j, carry):
            missed, sent = carry
            home = index[i, 0, HOP_LANE + j]
            stray = home >= 0
            used = counts[jnp.maximum(home, 0)]
            fits = stray & (used < HOPS)

            @pl.when(fits)
            def _():
                counts[home] = used + 1
                homes[sent] = home
                rows[sent] = used * BR
                pltpu.make_async_copy(
                    received.at[i, pl.ds(pl.multiple_of(j * BR, BR), BR)], staged.at[sent], sem
                ).start()
                target = index[i, 0, j].astype(jnp.float32)
                marks[home] = jnp.where(lane == used, target, marks[home])

            return (
                missed + jnp.where(stray & (used >= HOPS), 1, 0),
                sent + jnp.where(fits, 1, 0),
            )

        count = jnp.where(index[i, 0, STRAY_LANE] > 0, index[i, 0, COUNT_LANE], 0)
        return lax.fori_loop(0, count, slot, carry)

    missed, sent = lax.fori_loop(0, PEERS, source, (jnp.int32(0), jnp.int32(0)))
    write_tags(marks, tags, counts, None, missed, GROUPS)
    tag_copy = pltpu.make_async_copy(tags, out.at[:, pl.ds(HOPS * BR, LABEL_ROWS)], tag_sem)
    tag_copy.start()

    def arrive(i, carry):
        pltpu.make_async_copy(received.at[0, pl.ds(0, BR)], staged.at[0], sem).wait()
        return carry

    def leave(k, carry):
        row = pl.multiple_of(rows[k], BR)
        pltpu.make_async_copy(staged.at[k], out.at[homes[k], pl.ds(row, BR)], sem).start()
        return carry

    def left(k, carry):
        pltpu.make_async_copy(staged.at[0], out.at[0, pl.ds(0, BR)], sem).wait()
        return carry

    lax.fori_loop(0, sent, arrive, 0)
    lax.fori_loop(0, sent, leave, 0)
    lax.fori_loop(0, sent, left, 0)
    tag_copy.wait()


def forward(index, received):
    return pl.pallas_call(
        forward_kernel,
        out_shape=jax.ShapeDtypeStruct((GROUPS, HOPS * BR + LABEL_ROWS, 128), jnp.bfloat16),
        in_specs=[
            pl.BlockSpec(memory_space=pltpu.SMEM),
            pl.BlockSpec(memory_space=pl.ANY),
        ],
        out_specs=pl.BlockSpec(memory_space=pl.ANY),
        scratch_shapes=[
            pltpu.VMEM((GROUPS, 8, 128), jnp.float32),
            pltpu.VMEM((GROUPS, LABEL_ROWS, 128), jnp.bfloat16),
            pltpu.SMEM((GROUPS,), jnp.int32),
            pltpu.VMEM((GROUPS * HOPS, BR, 128), jnp.bfloat16),
            pltpu.SMEM((GROUPS * HOPS,), jnp.int32),
            pltpu.SMEM((GROUPS * HOPS,), jnp.int32),
            pltpu.SemaphoreType.DMA,
            pltpu.SemaphoreType.DMA,
        ],
        name="forward",
    )(index, received)


def target_of(target):
    chunk = target // OWNED
    row = target - chunk * OWNED
    return chunk, pl.multiple_of(row * BR + jnp.where(row >= 2, FLAG_ROWS, 0), 8)


def direct_kernel(index, received, out, total, landed, sems, sem):
    def fetch(i, at):
        def slot(j, spot):
            pltpu.make_async_copy(
                received.at[i, pl.ds(pl.multiple_of(j * BR, BR), BR)], landed.at[spot], sems.at[i]
            ).start()
            return spot + 1

        return lax.fori_loop(0, index[i, 0, COUNT_LANE], slot, at)

    lax.fori_loop(0, PEERS, fetch, jnp.int32(0))
    total[0:16] = jnp.zeros((16, CHUNK, 128), jnp.float32)

    def source(i, carry):
        missed, at = carry
        count = index[i, 0, COUNT_LANE]

        def arrive(j, carry):
            pltpu.make_async_copy(received.at[0, pl.ds(0, BR)], landed.at[0], sems.at[i]).wait()
            return carry

        lax.fori_loop(0, count, arrive, 0)

        def slot(j, spot):
            chunk, start = target_of(index[i, 0, j])
            chunk = jnp.where(index[i, 0, HOP_LANE + j] >= 0, 16, chunk)
            total[chunk, pl.ds(start, BR), :] += landed[spot].astype(jnp.float32)
            return spot + 1

        at = lax.fori_loop(0, count, slot, at)
        return missed + index[i, 0, OVER_LANE], at

    missed, _ = lax.fori_loop(0, PEERS, source, (jnp.int32(0), jnp.int32(0)))
    total[0:16, PIVOT_ROWS : PIVOT_ROWS + FLAG_ROWS, :] = jnp.full(
        (16, FLAG_ROWS, 128), missed.astype(jnp.float32)
    )
    copy = pltpu.make_async_copy(total.at[pl.ds(0, 16)], out, sem)
    copy.start()
    copy.wait()


def add_direct(index, received):
    return pl.pallas_call(
        direct_kernel,
        out_shape=jax.ShapeDtypeStruct((16, CHUNK, 128), jnp.float32),
        in_specs=[
            pl.BlockSpec(memory_space=pltpu.SMEM),
            pl.BlockSpec(memory_space=pl.ANY),
        ],
        out_specs=pl.BlockSpec(memory_space=pltpu.HBM),
        scratch_shapes=[
            pltpu.VMEM((17, CHUNK, 128), jnp.float32),
            pltpu.VMEM((PEERS * SLOTS, BR, 128), jnp.bfloat16),
            pltpu.SemaphoreType.DMA((PEERS,)),
            pltpu.SemaphoreType.DMA,
        ],
        name="add_direct",
    )(index, received)


def late_kernel(labels, late, dense, out, blocks, sums, flags, targets, homes, sem, sum_sem):
    def fetch(i, carry):
        def slot(j, carry):
            at, kept = carry
            target = labels[i, 0, j]

            def match(k, found):
                return jnp.where(targets[k] == target, k, found)

            found = lax.fori_loop(0, kept, match, jnp.int32(-1))
            fresh = found < 0
            homes[at] = jnp.where(fresh, kept, found)
            pltpu.make_async_copy(
                late.at[i, pl.ds(pl.multiple_of(j * BR, BR), BR)], blocks.at[at], sem
            ).start()

            @pl.when(fresh)
            def _():
                targets[kept] = target
                chunk, start = target_of(target)
                pltpu.make_async_copy(
                    dense.at[chunk, pl.ds(start, BR)], sums.at[kept], sum_sem
                ).start()

            return at + 1, kept + jnp.where(fresh, 1, 0)

        at, kept, missed = carry
        at, kept = lax.fori_loop(0, labels[i, 0, COUNT_LANE], slot, (at, kept))
        return at, kept, missed + labels[i, 0, OVER_LANE]

    zero = jnp.int32(0)
    count, kept, missed = lax.fori_loop(0, GROUPS, fetch, (zero, zero, zero))

    def arrive_block(k, carry):
        pltpu.make_async_copy(late.at[0, pl.ds(0, BR)], blocks.at[0], sem).wait()
        return carry

    def arrive_sum(k, carry):
        pltpu.make_async_copy(dense.at[0, pl.ds(0, BR)], sums.at[0], sum_sem).wait()
        return carry

    lax.fori_loop(0, count, arrive_block, 0)
    lax.fori_loop(0, kept, arrive_sum, 0)

    def add(k, carry):
        sums[homes[k]] += blocks[k].astype(jnp.float32)
        return carry

    lax.fori_loop(0, count, add, 0)

    def leave(k, carry):
        chunk, start = target_of(targets[k])
        pltpu.make_async_copy(sums.at[k], out.at[chunk, pl.ds(start, BR)], sum_sem).start()
        return carry

    def left(k, carry):
        pltpu.make_async_copy(sums.at[0], out.at[0, pl.ds(0, BR)], sum_sem).wait()
        return carry

    lax.fori_loop(0, kept, leave, 0)

    @pl.when(missed > 0)
    def _():
        flags[...] = jnp.full(flags.shape, missed.astype(jnp.float32))
        mark = pltpu.make_async_copy(flags, out.at[:, pl.ds(PIVOT_ROWS, FLAG_ROWS)], sem)
        mark.start()
        mark.wait()

    lax.fori_loop(0, kept, left, 0)


def add_late(labels, late, dense):
    most = GROUPS * HOPS
    anywhere = pl.BlockSpec(memory_space=pl.ANY)
    in_hbm = pl.BlockSpec(memory_space=pltpu.HBM)
    return pl.pallas_call(
        late_kernel,
        out_shape=jax.ShapeDtypeStruct((16, CHUNK, 128), jnp.float32),
        in_specs=[pl.BlockSpec(memory_space=pltpu.SMEM), anywhere, in_hbm],
        out_specs=in_hbm,
        input_output_aliases={2: 0},
        scratch_shapes=[
            pltpu.VMEM((most, BR, 128), jnp.bfloat16),
            pltpu.VMEM((most, BR, 128), jnp.float32),
            pltpu.VMEM((16, FLAG_ROWS, 128), jnp.float32),
            pltpu.SMEM((most,), jnp.int32),
            pltpu.SMEM((most,), jnp.int32),
            pltpu.SemaphoreType.DMA,
            pltpu.SemaphoreType.DMA,
        ],
        name="add_late",
    )(labels, late, dense)


def solve_kernel(spot, pivots, rhs, *refs):
    lowers, inverses = refs[0:4], refs[4:8]
    owned, update, solved_out, update_out, lower, inverse, kept = refs[8:]
    chain_at = spot[0]
    live_count = pivots[0]
    for shift in range(4):
        block = (chain_at - shift) & 3
        lower[block] = lowers[shift][...]
        inverse[block] = inverses[shift][...]
    for block in range(4):
        rows = slice(block * 256, (block + 1) * 256)
        at = block * (PIVOT_ROWS + FLAG_ROWS)
        partial = rhs[at : at + PIVOT_ROWS, :]
        if block > 0:
            partial = partial - jnp.dot(
                lower[block, :, 0 : block * 256],
                kept[0 : block * 256, :],
                preferred_element_type=jnp.float32,
            )
        row = block * 256 + lax.broadcasted_iota(jnp.int32, (256, 128), 0)
        product = jnp.dot(
            inverse[block],
            partial,
            precision=lax.Precision.HIGHEST,
            preferred_element_type=jnp.float32,
        )
        here = jnp.where(row < live_count, product, 0.0)
        kept[rows, :] = here.astype(jnp.bfloat16)

        @pl.when(chain_at == block)
        def _():
            solved_out[...] = here

    update_out[...] = owned[PIVOT_ROWS + FLAG_ROWS :, :] - jnp.dot(
        update[...], kept[...], preferred_element_type=jnp.float32
    )


def solve(spot, pivots, rhs, lowers, inverses, owned, update):
    smem = pl.BlockSpec(memory_space=pltpu.SMEM)
    vmem = pl.BlockSpec(memory_space=pltpu.VMEM)
    return pl.pallas_call(
        solve_kernel,
        out_shape=(
            jax.ShapeDtypeStruct((256, 128), jnp.float32),
            jax.ShapeDtypeStruct((512, 128), jnp.float32),
        ),
        in_specs=[smem, smem] + [vmem] * 11,
        out_specs=(vmem, vmem),
        scratch_shapes=[
            pltpu.VMEM((4, 256, 768), jnp.bfloat16),
            pltpu.VMEM((4, 256, 256), jnp.float32),
            pltpu.VMEM((1024, 128), jnp.bfloat16),
        ],
        compiler_params=pltpu.CompilerParams(vmem_limit_bytes=20 << 20),
        name="solve",
    )(spot, pivots, rhs, *lowers, *inverses, owned, update)


def around_chain(value):
    moved = [
        lax.ppermute(value, "chain", [(i, (i + shift) % 4) for i in range(4)])
        for shift in (1, 2, 3)
    ]
    return (value, *moved)


def labels_of(received):
    return received[:, -LABEL_ROWS : 1 - LABEL_ROWS, :].astype(jnp.int32)


def body(
    rhs, child_blocks, dest_front, dest_place, front_pivots, diag_inv, lower_factor, update_factor
):
    fronts = dest_front.reshape(-1)
    spot = lax.axis_index("chain").astype(jnp.int32).reshape(1)
    turn = lax.axis_index(LINE).astype(jnp.int32).reshape(1) + 2 * spot
    packed = pack(turn, fronts, dest_place, child_blocks)
    received = lax.all_to_all(packed, SLAB, split_axis=0, concat_axis=0, tiled=True)
    padded = jnp.pad(rhs, ((0, FLAG_ROWS), (0, 0)))
    received, padded = lax.optimization_barrier((received, padded))
    index = labels_of(received)
    late = lax.all_to_all(forward(index, received), LINE, split_axis=0, concat_axis=0, tiled=True)
    dense = add_late(labels_of(late), late, add_direct(index, received))
    dense, lower_factor, diag_inv = lax.optimization_barrier((dense, lower_factor, diag_inv))
    owned = lax.psum_scatter(dense, "z", scatter_dimension=0, tiled=True)
    lowers = around_chain(lower_factor)
    inverses = around_chain(diag_inv)
    owned, lowers, inverses = lax.optimization_barrier((owned, lowers, inverses))
    owned = owned.reshape(CHUNK, 128)

    def share(mine):
        return lax.all_gather(
            padded + mine[: PIVOT_ROWS + FLAG_ROWS], "chain", axis=0, tiled=True
        )

    def finish(all_rhs, mine, lowers, inverses):
        return solve(spot, front_pivots, all_rhs, lowers, inverses, mine, update_factor)

    def general(*fast):
        blocks = full_exchange(child_blocks, fronts, dest_place).reshape(OWNED * BR, 128)
        flags = jnp.zeros((FLAG_ROWS, 128), jnp.float32)
        mine = jnp.concatenate([blocks[:PIVOT_ROWS], flags, blocks[PIVOT_ROWS:]])
        factors = around_chain(lower_factor), around_chain(diag_inv)
        return finish(share(mine), mine, *factors)

    all_rhs = share(owned)
    over = jnp.sum(all_rhs.reshape(4, PIVOT_ROWS + FLAG_ROWS, 128)[:, PIVOT_ROWS, 0])
    fast = finish(all_rhs, owned, lowers, inverses)
    return lax.cond(over > 0, general, lambda *fast: fast, *fast)


def solution(mesh):
    grid = Mesh(mesh.devices.reshape(4, 16, 2, 4), ALL)
    rows = P(ALL, None)
    return jax.shard_map(
        body,
        mesh=grid,
        in_specs=(rows, P(ALL, None, None), rows, P(ALL), P(FRONT), rows, rows, rows),
        out_specs=(rows, rows),
        check_vma=False,
    )
```

```python
import jax
import jax.numpy as jnp
from jax import lax
from jax.experimental import pallas as pl
from jax.experimental.pallas import tpu as pltpu
from jax.sharding import Mesh, PartitionSpec as P

BR = 128
FRONT = ("x", "z", "core")
ALL = ("x", "z", "core", "chain")
SLAB = ("x", "core", "chain")
LINE = ("x", "core")
SLOTS = 5
HOPS = 5
PEERS = 32
GROUPS = 8
LABEL_ROWS = 16
OWNED = 6
HOP_LANE = 64
STRAY_LANE = 125
COUNT_LANE = 126
OVER_LANE = 127
PIVOT_ROWS = 256
MARK_ROWS = 8
MARK = 1e30
LIMIT = 1e20
CHUNK = OWNED * BR


def slot_table(blocks, fronts, places, dest_count, slot_width):
    block_count = fronts.shape[0]
    sequence = jnp.arange(block_count, dtype=jnp.int32)
    earlier = (fronts[None, :] == fronts[:, None]) & (sequence[None, :] < sequence[:, None])
    rank_of = jnp.sum(earlier.astype(jnp.int32), axis=1)
    target = fronts * slot_width + rank_of
    source = jnp.full((dest_count * slot_width,), block_count, jnp.int32).at[target].set(sequence)
    slot_data = jnp.take(blocks, source, axis=0, mode="fill", fill_value=0)
    labels = jnp.take(places, source, axis=0, mode="fill", fill_value=-1)
    return (
        slot_data.reshape((dest_count, slot_width) + blocks.shape[1:]),
        labels.reshape(dest_count, slot_width),
    )


def full_exchange(child_blocks, fronts, places):
    slot_data, labels = slot_table(child_blocks, fronts, places, 128, 2)
    received = lax.all_to_all(slot_data, FRONT, split_axis=0, concat_axis=0, tiled=True)
    tags = lax.all_to_all(labels, FRONT, split_axis=0, concat_axis=0, tiled=True).reshape(-1)
    placed = jnp.where(
        tags < 8, tags // 2 * OWNED + tags % 2, (tags - 8) // 4 * OWNED + 2 + (tags - 8) % 4
    )
    placed = jnp.where(tags < 0, -1, placed)
    row_ids = jnp.arange(4 * OWNED, dtype=jnp.int32)
    onehot = (placed[None, :] == row_ids[:, None]).astype(jnp.bfloat16)
    flattened = received.reshape((-1,) + received.shape[2:])
    merged = jnp.einsum("km,mrs->krs", onehot, flattened, preferred_element_type=jnp.float32)
    return lax.psum_scatter(merged, "chain", scatter_dimension=0, tiled=True)


def write_tags(marks, tags, counts, strays, missed, count):
    lane = lax.broadcasted_iota(jnp.int32, (8, 128), 1)
    for peer in range(count):
        row = jnp.where(lane == COUNT_LANE, counts[peer].astype(jnp.float32), marks[peer])
        if strays is not None:
            row = jnp.where(lane == STRAY_LANE, strays[peer].astype(jnp.float32), row)
        row = jnp.where(lane == OVER_LANE, missed.astype(jnp.float32), row)
        tags[peer, 0:8, :] = row.astype(jnp.bfloat16)
        tags[peer, 8:16, :] = row.astype(jnp.bfloat16)


def send_kernel(
    spot, front, place, source, out, marks, tags, counts, strays, seen, late, slots, blocks, sem, tag_sem, in_sem
):
    load = pltpu.make_async_copy(source, blocks, in_sem)
    load.start()
    for peer in range(PEERS):
        counts[peer] = 0
        strays[peer] = 0
        seen[peer] = 0
    marks[...] = jnp.full(marks.shape, -1.0, jnp.float32)
    lane = lax.broadcasted_iota(jnp.int32, (8, 128), 1)

    def route(i):
        where_front = front[i]
        target = place[i]
        pivot = target < 8
        owner = jnp.where(pivot, target >> 1, (target - 8) >> 2)
        peer = ((where_front >> 5) * 2 + (where_front & 1)) * 4 + owner
        index = ((where_front >> 1) & 15) * OWNED + jnp.where(
            pivot, target & 1, 2 + ((target - 8) & 3)
        )
        live = target >= 0
        return live, jnp.where(live, peer, 0), index

    def launch(i, carry):
        peer = slots[i] >> 3
        used = slots[i] & 7

        @pl.when(slots[i] >= 0)
        def _():
            pltpu.make_async_copy(
                blocks.at[i], out.at[peer, pl.ds(pl.multiple_of(used * BR, BR), BR)], sem
            ).start()

        return carry

    def direct(i, carry):
        left, sent = carry
        live, peer, index = route(i)
        used = counts[peer]
        fits = live & (used < SLOTS)
        slots[i] = -1

        @pl.when(fits)
        def _():
            counts[peer] = used + 1
            slots[i] = (peer << 3) + used
            marks[peer] = jnp.where(lane == used, index.astype(jnp.float32), marks[peer])

        @pl.when(live & (used >= SLOTS))
        def _():
            late[left] = i

        return (
            left + jnp.where(live & (used >= SLOTS), 1, 0),
            sent + jnp.where(fits, 1, 0),
        )

    left, sent = lax.fori_loop(0, front.shape[0], direct, (jnp.int32(0), jnp.int32(0)))

    def detour(k, carry):
        missed, sent = carry
        i = late[k]
        _, home, index = route(i)
        group = home >> 2
        first = spot[0] + 3 * seen[home]
        seen[home] = seen[home] + 1
        chosen = jnp.int32(-1)
        for h in reversed(range(GROUPS - 1)):
            turn = lax.rem(first + h, GROUPS - 1)
            peer = (((group + 1 + turn) & 7) << 2) + (home & 3)
            chosen = jnp.where(counts[peer] < SLOTS, peer, chosen)
        fits = chosen >= 0

        @pl.when(fits)
        def _():
            used = counts[chosen]
            counts[chosen] = used + 1
            strays[chosen] = strays[chosen] + 1
            slots[i] = (chosen << 3) + used
            row = jnp.where(lane == used, index.astype(jnp.float32), marks[chosen])
            marks[chosen] = jnp.where(lane == HOP_LANE + used, group.astype(jnp.float32), row)

        return missed + jnp.where(fits, 0, 1), sent + jnp.where(fits, 1, 0)

    missed, sent = lax.fori_loop(0, left, detour, (jnp.int32(0), sent))
    load.wait()
    lax.fori_loop(0, front.shape[0], launch, 0)
    write_tags(marks, tags, counts, strays, missed, PEERS)
    tag_copy = pltpu.make_async_copy(tags, out.at[:, pl.ds(SLOTS * BR, LABEL_ROWS)], tag_sem)
    tag_copy.start()

    def drain(i, carry):
        pltpu.make_async_copy(blocks.at[0], out.at[0, pl.ds(0, BR)], sem).wait()
        return carry

    lax.fori_loop(0, sent, drain, 0)
    tag_copy.wait()


def pack(turn, fronts, places, blocks):
    smem = pl.BlockSpec(memory_space=pltpu.SMEM)
    return pl.pallas_call(
        send_kernel,
        out_shape=jax.ShapeDtypeStruct((PEERS, SLOTS * BR + LABEL_ROWS, 128), jnp.bfloat16),
        in_specs=[smem, smem, smem, pl.BlockSpec(memory_space=pl.ANY)],
        out_specs=pl.BlockSpec(memory_space=pl.ANY),
        scratch_shapes=[
            pltpu.VMEM((PEERS, 8, 128), jnp.float32),
            pltpu.VMEM((PEERS, LABEL_ROWS, 128), jnp.bfloat16),
            pltpu.SMEM((PEERS,), jnp.int32),
            pltpu.SMEM((PEERS,), jnp.int32),
            pltpu.SMEM((PEERS,), jnp.int32),
            pltpu.SMEM((128,), jnp.int32),
            pltpu.SMEM((128,), jnp.int32),
            pltpu.VMEM(blocks.shape, jnp.bfloat16),
            pltpu.SemaphoreType.DMA,
            pltpu.SemaphoreType.DMA,
            pltpu.SemaphoreType.DMA,
        ],
        name="pack",
    )(turn, fronts, places, blocks)


def forward_kernel(index, received, out, marks, tags, counts, staged, homes, rows, sem, tag_sem):
    for peer in range(GROUPS):
        counts[peer] = 0
    marks[...] = jnp.full(marks.shape, -1.0, jnp.float32)
    lane = lax.broadcasted_iota(jnp.int32, (8, 128), 1)

    def source(i, carry):
        def slot(j, carry):
            missed, sent = carry
            home = index[i, 0, HOP_LANE + j]
            stray = home >= 0
            used = counts[jnp.maximum(home, 0)]
            fits = stray & (used < HOPS)

            @pl.when(fits)
            def _():
                counts[home] = used + 1
                homes[sent] = home
                rows[sent] = used * BR
                pltpu.make_async_copy(
                    received.at[i, pl.ds(pl.multiple_of(j * BR, BR), BR)], staged.at[sent], sem
                ).start()
                target = index[i, 0, j].astype(jnp.float32)
                marks[home] = jnp.where(lane == used, target, marks[home])

            return (
                missed + jnp.where(stray & (used >= HOPS), 1, 0),
                sent + jnp.where(fits, 1, 0),
            )

        count = jnp.where(index[i, 0, STRAY_LANE] > 0, index[i, 0, COUNT_LANE], 0)
        return lax.fori_loop(0, count, slot, carry)

    missed, sent = lax.fori_loop(0, PEERS, source, (jnp.int32(0), jnp.int32(0)))
    write_tags(marks, tags, counts, None, missed, GROUPS)
    tag_copy = pltpu.make_async_copy(tags, out.at[:, pl.ds(HOPS * BR, LABEL_ROWS)], tag_sem)
    tag_copy.start()

    def arrive(i, carry):
        pltpu.make_async_copy(received.at[0, pl.ds(0, BR)], staged.at[0], sem).wait()
        return carry

    def leave(k, carry):
        row = pl.multiple_of(rows[k], BR)
        pltpu.make_async_copy(staged.at[k], out.at[homes[k], pl.ds(row, BR)], sem).start()
        return carry

    def left(k, carry):
        pltpu.make_async_copy(staged.at[0], out.at[0, pl.ds(0, BR)], sem).wait()
        return carry

    lax.fori_loop(0, sent, arrive, 0)
    lax.fori_loop(0, sent, leave, 0)
    lax.fori_loop(0, sent, left, 0)
    tag_copy.wait()


def forward(index, received):
    return pl.pallas_call(
        forward_kernel,
        out_shape=jax.ShapeDtypeStruct((GROUPS, HOPS * BR + LABEL_ROWS, 128), jnp.bfloat16),
        in_specs=[
            pl.BlockSpec(memory_space=pltpu.SMEM),
            pl.BlockSpec(memory_space=pl.ANY),
        ],
        out_specs=pl.BlockSpec(memory_space=pl.ANY),
        scratch_shapes=[
            pltpu.VMEM((GROUPS, 8, 128), jnp.float32),
            pltpu.VMEM((GROUPS, LABEL_ROWS, 128), jnp.bfloat16),
            pltpu.SMEM((GROUPS,), jnp.int32),
            pltpu.VMEM((GROUPS * HOPS, BR, 128), jnp.bfloat16),
            pltpu.SMEM((GROUPS * HOPS,), jnp.int32),
            pltpu.SMEM((GROUPS * HOPS,), jnp.int32),
            pltpu.SemaphoreType.DMA,
            pltpu.SemaphoreType.DMA,
        ],
        name="forward",
    )(index, received)


def target_of(target):
    chunk = target // OWNED
    row = target - chunk * OWNED
    return chunk, pl.multiple_of(row * BR, BR)


def direct_kernel(spot, index, received, rhs, out, total, landed, sems, sem):
    def fetch(i, at):
        def slot(j, spot):
            pltpu.make_async_copy(
                received.at[i, pl.ds(pl.multiple_of(j * BR, BR), BR)], landed.at[spot], sems.at[i]
            ).start()
            return spot + 1

        return lax.fori_loop(0, index[i, 0, COUNT_LANE], slot, at)

    lax.fori_loop(0, PEERS, fetch, jnp.int32(0))
    total[0:16] = jnp.zeros((16, CHUNK, 128), jnp.float32)
    total[spot[0], 0:PIVOT_ROWS, :] = rhs[...]

    def source(i, carry):
        missed, at = carry
        count = index[i, 0, COUNT_LANE]

        def arrive(j, carry):
            pltpu.make_async_copy(received.at[0, pl.ds(0, BR)], landed.at[0], sems.at[i]).wait()
            return carry

        lax.fori_loop(0, count, arrive, 0)

        def slot(j, spot):
            chunk, start = target_of(index[i, 0, j])
            chunk = jnp.where(index[i, 0, HOP_LANE + j] >= 0, 16, chunk)
            total[chunk, pl.ds(start, BR), :] += landed[spot].astype(jnp.float32)
            return spot + 1

        at = lax.fori_loop(0, count, slot, at)
        return missed + index[i, 0, OVER_LANE], at

    missed, _ = lax.fori_loop(0, PEERS, source, (jnp.int32(0), jnp.int32(0)))

    @pl.when(missed > 0)
    def _():
        total[0:16, 0:MARK_ROWS, :] = jnp.full((16, MARK_ROWS, 128), MARK, jnp.float32)

    copy = pltpu.make_async_copy(total.at[pl.ds(0, 16)], out, sem)
    copy.start()
    copy.wait()


def add_direct(spot, index, received, rhs):
    return pl.pallas_call(
        direct_kernel,
        out_shape=jax.ShapeDtypeStruct((16, CHUNK, 128), jnp.float32),
        in_specs=[
            pl.BlockSpec(memory_space=pltpu.SMEM),
            pl.BlockSpec(memory_space=pltpu.SMEM),
            pl.BlockSpec(memory_space=pl.ANY),
            pl.BlockSpec(memory_space=pltpu.VMEM),
        ],
        out_specs=pl.BlockSpec(memory_space=pltpu.HBM),
        scratch_shapes=[
            pltpu.VMEM((17, CHUNK, 128), jnp.float32),
            pltpu.VMEM((PEERS * SLOTS, BR, 128), jnp.bfloat16),
            pltpu.SemaphoreType.DMA((PEERS,)),
            pltpu.SemaphoreType.DMA,
        ],
        name="add_direct",
    )(spot, index, received, rhs)


def late_kernel(labels, late, dense, out, blocks, sums, flags, targets, homes, sem, sum_sem):
    def fetch(i, carry):
        def slot(j, carry):
            at, kept = carry
            target = labels[i, 0, j]

            def match(k, found):
                return jnp.where(targets[k] == target, k, found)

            found = lax.fori_loop(0, kept, match, jnp.int32(-1))
            fresh = found < 0
            homes[at] = jnp.where(fresh, kept, found)
            pltpu.make_async_copy(
                late.at[i, pl.ds(pl.multiple_of(j * BR, BR), BR)], blocks.at[at], sem
            ).start()

            @pl.when(fresh)
            def _():
                targets[kept] = target
                chunk, start = target_of(target)
                pltpu.make_async_copy(
                    dense.at[chunk, pl.ds(start, BR)], sums.at[kept], sum_sem
                ).start()

            return at + 1, kept + jnp.where(fresh, 1, 0)

        at, kept, missed = carry
        at, kept = lax.fori_loop(0, labels[i, 0, COUNT_LANE], slot, (at, kept))
        return at, kept, missed + labels[i, 0, OVER_LANE]

    zero = jnp.int32(0)
    count, kept, missed = lax.fori_loop(0, GROUPS, fetch, (zero, zero, zero))

    def arrive_block(k, carry):
        pltpu.make_async_copy(late.at[0, pl.ds(0, BR)], blocks.at[0], sem).wait()
        return carry

    def arrive_sum(k, carry):
        pltpu.make_async_copy(dense.at[0, pl.ds(0, BR)], sums.at[0], sum_sem).wait()
        return carry

    lax.fori_loop(0, count, arrive_block, 0)
    lax.fori_loop(0, kept, arrive_sum, 0)

    def add(k, carry):
        sums[homes[k]] += blocks[k].astype(jnp.float32)
        return carry

    lax.fori_loop(0, count, add, 0)

    def leave(k, carry):
        chunk, start = target_of(targets[k])
        pltpu.make_async_copy(sums.at[k], out.at[chunk, pl.ds(start, BR)], sum_sem).start()
        return carry

    def left(k, carry):
        pltpu.make_async_copy(sums.at[0], out.at[0, pl.ds(0, BR)], sum_sem).wait()
        return carry

    lax.fori_loop(0, kept, leave, 0)
    lax.fori_loop(0, kept, left, 0)

    @pl.when(missed > 0)
    def _():
        flags[...] = jnp.full(flags.shape, MARK, jnp.float32)
        mark = pltpu.make_async_copy(flags, out.at[:, pl.ds(0, MARK_ROWS)], sem)
        mark.start()
        mark.wait()


def add_late(labels, late, dense):
    most = GROUPS * HOPS
    anywhere = pl.BlockSpec(memory_space=pl.ANY)
    in_hbm = pl.BlockSpec(memory_space=pltpu.HBM)
    return pl.pallas_call(
        late_kernel,
        out_shape=jax.ShapeDtypeStruct((16, CHUNK, 128), jnp.float32),
        in_specs=[pl.BlockSpec(memory_space=pltpu.SMEM), anywhere, in_hbm],
        out_specs=in_hbm,
        input_output_aliases={2: 0},
        scratch_shapes=[
            pltpu.VMEM((most, BR, 128), jnp.bfloat16),
            pltpu.VMEM((most, BR, 128), jnp.float32),
            pltpu.VMEM((16, MARK_ROWS, 128), jnp.float32),
            pltpu.SMEM((most,), jnp.int32),
            pltpu.SMEM((most,), jnp.int32),
            pltpu.SemaphoreType.DMA,
            pltpu.SemaphoreType.DMA,
        ],
        name="add_late",
    )(labels, late, dense)


def solve_kernel(spot, pivots, rhs, *refs):
    lowers, inverses = refs[0:4], refs[4:8]
    owned, update, solved_out, update_out, lower, inverse, start, sem = refs[8:]
    fetch = pltpu.make_async_copy(owned.at[pl.ds(PIVOT_ROWS, CHUNK - PIVOT_ROWS)], start, sem)
    fetch.start()
    chain_at = spot[0]
    live_count = pivots[0]
    for shift in range(4):
        block = (chain_at - shift) & 3
        lower[block] = lowers[shift][...]
        inverse[block] = inverses[shift][...]
    partials = [rhs[block * PIVOT_ROWS : (block + 1) * PIVOT_ROWS, :] for block in range(4)]
    products = []
    for block in range(4):
        row = block * PIVOT_ROWS + lax.broadcasted_iota(jnp.int32, (PIVOT_ROWS, 128), 0)
        product = jnp.dot(
            inverse[block],
            partials[block],
            precision=lax.Precision.HIGHEST,
            preferred_element_type=jnp.float32,
        )
        here = jnp.where(row < live_count, product, 0.0)
        kept = here.astype(jnp.bfloat16)
        columns = slice(block * PIVOT_ROWS, (block + 1) * PIVOT_ROWS)
        for later in range(block + 1, 4):
            partials[later] = partials[later] - jnp.dot(
                lower[later, :, columns], kept, preferred_element_type=jnp.float32
            )
        products.append(jnp.dot(update[:, columns], kept, preferred_element_type=jnp.float32))

        @pl.when(chain_at == block)
        def _():
            solved_out[...] = here

    fetch.wait()
    update_out[...] = start[...] - ((products[0] + products[1]) + (products[2] + products[3]))


def solve(spot, pivots, rhs, lowers, inverses, owned, update):
    smem = pl.BlockSpec(memory_space=pltpu.SMEM)
    vmem = pl.BlockSpec(memory_space=pltpu.VMEM)
    return pl.pallas_call(
        solve_kernel,
        out_shape=(
            jax.ShapeDtypeStruct((PIVOT_ROWS, 128), jnp.float32),
            jax.ShapeDtypeStruct((CHUNK - PIVOT_ROWS, 128), jnp.float32),
        ),
        in_specs=[smem, smem] + [vmem] * 9 + [pl.BlockSpec(memory_space=pltpu.HBM), vmem],
        out_specs=(vmem, vmem),
        scratch_shapes=[
            pltpu.VMEM((4, PIVOT_ROWS, 3 * PIVOT_ROWS), jnp.bfloat16),
            pltpu.VMEM((4, PIVOT_ROWS, PIVOT_ROWS), jnp.float32),
            pltpu.VMEM((CHUNK - PIVOT_ROWS, 128), jnp.float32),
            pltpu.SemaphoreType.DMA,
        ],
        compiler_params=pltpu.CompilerParams(vmem_limit_bytes=20 << 20),
        name="solve",
    )(spot, pivots, rhs, *lowers, *inverses, owned, update)


def around_chain(value):
    moved = [
        lax.ppermute(value, "chain", [(i, (i + shift) % 4) for i in range(4)])
        for shift in (1, 2, 3)
    ]
    return (value, *moved)


def labels_of(received):
    return received[:, -LABEL_ROWS : 1 - LABEL_ROWS, :].astype(jnp.int32)


def body(
    rhs, child_blocks, dest_front, dest_place, front_pivots, diag_inv, lower_factor, update_factor
):
    fronts = dest_front.reshape(-1)
    spot = lax.axis_index("chain").astype(jnp.int32).reshape(1)
    turn = lax.axis_index(LINE).astype(jnp.int32).reshape(1) + 2 * spot
    packed = pack(turn, fronts, dest_place, child_blocks)
    received = lax.all_to_all(packed, SLAB, split_axis=0, concat_axis=0, tiled=True)
    index = labels_of(received)
    late = lax.all_to_all(forward(index, received), LINE, split_axis=0, concat_axis=0, tiled=True)
    height = lax.axis_index("z").astype(jnp.int32).reshape(1)
    dense = add_late(labels_of(late), late, add_direct(height, index, received, rhs))
    dense, lower_factor, diag_inv = lax.optimization_barrier((dense, lower_factor, diag_inv))
    owned = lax.psum_scatter(dense, "z", scatter_dimension=0, tiled=True)
    lowers = around_chain(lower_factor)
    inverses = around_chain(diag_inv)
    owned, lowers, inverses = lax.optimization_barrier((owned, lowers, inverses))
    owned = owned.reshape(CHUNK, 128)

    def share(mine):
        copies = jnp.broadcast_to(mine, (4, PIVOT_ROWS, 128))
        spread = lax.all_to_all(copies, "chain", split_axis=0, concat_axis=0, tiled=True)
        return spread.reshape(4 * PIVOT_ROWS, 128)

    def finish(all_rhs, mine, lowers, inverses):
        return solve(spot, front_pivots, all_rhs, lowers, inverses, mine, update_factor)

    def general(*fast):
        mine = full_exchange(child_blocks, fronts, dest_place).reshape(CHUNK, 128)
        factors = around_chain(lower_factor), around_chain(diag_inv)
        return finish(share(rhs + mine[:PIVOT_ROWS]), mine, *factors)

    all_rhs = share(owned[:PIVOT_ROWS])
    over = jnp.max(all_rhs.reshape(4, PIVOT_ROWS, 128)[:, 0, 0])
    fast = finish(all_rhs, owned, lowers, inverses)
    return lax.cond(over > LIMIT, general, lambda *fast: fast, *fast)


def solution(mesh):
    grid = Mesh(mesh.devices.reshape(4, 16, 2, 4), ALL)
    rows = P(ALL, None)
    return jax.shard_map(
        body,
        mesh=grid,
        in_specs=(rows, P(ALL, None, None), rows, P(ALL), P(FRONT), rows, rows, rows),
        out_specs=(rows, rows),
        check_vma=False,
    )
```

```python
import jax
import jax.numpy as jnp
from jax import lax
from jax.experimental import pallas as pl
from jax.experimental.pallas import tpu as pltpu
from jax.sharding import Mesh, PartitionSpec as P

BR = 128
FRONT = ("x", "z", "core")
ALL = ("x", "z", "core", "chain")
SLAB = ("x", "core", "chain")
LINE = ("x", "core")
SLOTS = 5
HOPS = 5
PEERS = 32
GROUPS = 8
LABEL_ROWS = 8
OWNED = 6
HOP_LANE = 64
STRAY_LANE = 125
COUNT_LANE = 126
OVER_LANE = 127
PIVOT_ROWS = 256
MARK_ROWS = 8
MARK = 1e30
LIMIT = 1e20
CHUNK = OWNED * BR


def slot_table(blocks, fronts, places, dest_count, slot_width):
    block_count = fronts.shape[0]
    sequence = jnp.arange(block_count, dtype=jnp.int32)
    earlier = (fronts[None, :] == fronts[:, None]) & (sequence[None, :] < sequence[:, None])
    rank_of = jnp.sum(earlier.astype(jnp.int32), axis=1)
    target = fronts * slot_width + rank_of
    source = jnp.full((dest_count * slot_width,), block_count, jnp.int32).at[target].set(sequence)
    slot_data = jnp.take(blocks, source, axis=0, mode="fill", fill_value=0)
    labels = jnp.take(places, source, axis=0, mode="fill", fill_value=-1)
    return (
        slot_data.reshape((dest_count, slot_width) + blocks.shape[1:]),
        labels.reshape(dest_count, slot_width),
    )


def full_exchange(child_blocks, fronts, places):
    slot_data, labels = slot_table(child_blocks, fronts, places, 128, 2)
    received = lax.all_to_all(slot_data, FRONT, split_axis=0, concat_axis=0, tiled=True)
    tags = lax.all_to_all(labels, FRONT, split_axis=0, concat_axis=0, tiled=True).reshape(-1)
    placed = jnp.where(
        tags < 8, tags // 2 * OWNED + tags % 2, (tags - 8) // 4 * OWNED + 2 + (tags - 8) % 4
    )
    placed = jnp.where(tags < 0, -1, placed)
    row_ids = jnp.arange(4 * OWNED, dtype=jnp.int32)
    onehot = (placed[None, :] == row_ids[:, None]).astype(jnp.bfloat16)
    flattened = received.reshape((-1,) + received.shape[2:])
    merged = jnp.einsum("km,mrs->krs", onehot, flattened, preferred_element_type=jnp.float32)
    return lax.psum_scatter(merged, "chain", scatter_dimension=0, tiled=True)


def write_tags(marks, tags, counts, strays, missed, count):
    lane = lax.broadcasted_iota(jnp.int32, (8, 128), 1)
    for peer in range(count):
        row = jnp.where(lane == COUNT_LANE, counts[peer].astype(jnp.float32), marks[peer])
        if strays is not None:
            row = jnp.where(lane == STRAY_LANE, strays[peer].astype(jnp.float32), row)
        row = jnp.where(lane == OVER_LANE, missed.astype(jnp.float32), row)
        tags[peer] = row.astype(jnp.bfloat16)


def send_kernel(
    spot, front, place, source, out, marks, tags, counts, strays, seen, late, slots, blocks, sem, tag_sem, in_sem
):
    load = pltpu.make_async_copy(source, blocks, in_sem)
    load.start()
    for peer in range(PEERS):
        counts[peer] = 0
        strays[peer] = 0
        seen[peer] = 0
    marks[...] = jnp.full(marks.shape, -1.0, jnp.float32)
    lane = lax.broadcasted_iota(jnp.int32, (8, 128), 1)

    def route(i):
        where_front = front[i]
        target = place[i]
        pivot = target < 8
        owner = jnp.where(pivot, target >> 1, (target - 8) >> 2)
        peer = ((where_front >> 5) * 2 + (where_front & 1)) * 4 + owner
        index = ((where_front >> 1) & 15) * OWNED + jnp.where(
            pivot, target & 1, 2 + ((target - 8) & 3)
        )
        live = target >= 0
        return live, jnp.where(live, peer, 0), index

    def launch(i, carry):
        peer = slots[i] >> 3
        used = slots[i] & 7

        @pl.when(slots[i] >= 0)
        def _():
            pltpu.make_async_copy(
                blocks.at[i], out.at[peer, pl.ds(pl.multiple_of(used * BR, BR), BR)], sem
            ).start()

        return carry

    def direct(i, carry):
        left, sent = carry
        live, peer, index = route(i)
        used = counts[peer]
        fits = live & (used < SLOTS)
        slots[i] = -1

        @pl.when(fits)
        def _():
            counts[peer] = used + 1
            slots[i] = (peer << 3) + used
            marks[peer] = jnp.where(lane == used, index.astype(jnp.float32), marks[peer])

        @pl.when(live & (used >= SLOTS))
        def _():
            late[left] = i

        return (
            left + jnp.where(live & (used >= SLOTS), 1, 0),
            sent + jnp.where(fits, 1, 0),
        )

    left, sent = lax.fori_loop(0, front.shape[0], direct, (jnp.int32(0), jnp.int32(0)))

    def detour(k, carry):
        missed, sent = carry
        i = late[k]
        _, home, index = route(i)
        group = home >> 2
        first = spot[0] + 3 * seen[home]
        seen[home] = seen[home] + 1
        chosen = jnp.int32(-1)
        for h in reversed(range(GROUPS - 1)):
            turn = lax.rem(first + h, GROUPS - 1)
            peer = (((group + 1 + turn) & 7) << 2) + (home & 3)
            chosen = jnp.where(counts[peer] < SLOTS, peer, chosen)
        fits = chosen >= 0

        @pl.when(fits)
        def _():
            used = counts[chosen]
            counts[chosen] = used + 1
            strays[chosen] = strays[chosen] + 1
            slots[i] = (chosen << 3) + used
            row = jnp.where(lane == used, index.astype(jnp.float32), marks[chosen])
            marks[chosen] = jnp.where(lane == HOP_LANE + used, group.astype(jnp.float32), row)

        return missed + jnp.where(fits, 0, 1), sent + jnp.where(fits, 1, 0)

    missed, sent = lax.fori_loop(0, left, detour, (jnp.int32(0), sent))
    load.wait()
    lax.fori_loop(0, front.shape[0], launch, 0)
    write_tags(marks, tags, counts, strays, missed, PEERS)
    tag_copy = pltpu.make_async_copy(tags, out.at[:, pl.ds(SLOTS * BR, LABEL_ROWS)], tag_sem)
    tag_copy.start()

    def drain(i, carry):
        pltpu.make_async_copy(blocks.at[0], out.at[0, pl.ds(0, BR)], sem).wait()
        return carry

    lax.fori_loop(0, sent, drain, 0)
    tag_copy.wait()


def pack(turn, fronts, places, blocks):
    smem = pl.BlockSpec(memory_space=pltpu.SMEM)
    return pl.pallas_call(
        send_kernel,
        out_shape=jax.ShapeDtypeStruct((PEERS, SLOTS * BR + LABEL_ROWS, 128), jnp.bfloat16),
        in_specs=[smem, smem, smem, pl.BlockSpec(memory_space=pl.ANY)],
        out_specs=pl.BlockSpec(memory_space=pl.ANY),
        scratch_shapes=[
            pltpu.VMEM((PEERS, 8, 128), jnp.float32),
            pltpu.VMEM((PEERS, LABEL_ROWS, 128), jnp.bfloat16),
            pltpu.SMEM((PEERS,), jnp.int32),
            pltpu.SMEM((PEERS,), jnp.int32),
            pltpu.SMEM((PEERS,), jnp.int32),
            pltpu.SMEM((128,), jnp.int32),
            pltpu.SMEM((128,), jnp.int32),
            pltpu.VMEM(blocks.shape, jnp.bfloat16),
            pltpu.SemaphoreType.DMA,
            pltpu.SemaphoreType.DMA,
            pltpu.SemaphoreType.DMA,
        ],
        name="pack",
    )(turn, fronts, places, blocks)


def forward_kernel(index, received, out, marks, tags, counts, staged, homes, rows, sem, tag_sem):
    for peer in range(GROUPS):
        counts[peer] = 0
    marks[...] = jnp.full(marks.shape, -1.0, jnp.float32)
    lane = lax.broadcasted_iota(jnp.int32, (8, 128), 1)

    def source(i, carry):
        def slot(j, carry):
            missed, sent = carry
            home = index[i, 0, HOP_LANE + j]
            stray = home >= 0
            used = counts[jnp.maximum(home, 0)]
            fits = stray & (used < HOPS)

            @pl.when(fits)
            def _():
                counts[home] = used + 1
                homes[sent] = home
                rows[sent] = used * BR
                pltpu.make_async_copy(
                    received.at[i, pl.ds(pl.multiple_of(j * BR, BR), BR)], staged.at[sent], sem
                ).start()
                target = index[i, 0, j].astype(jnp.float32)
                marks[home] = jnp.where(lane == used, target, marks[home])

            return (
                missed + jnp.where(stray & (used >= HOPS), 1, 0),
                sent + jnp.where(fits, 1, 0),
            )

        count = jnp.where(index[i, 0, STRAY_LANE] > 0, index[i, 0, COUNT_LANE], 0)
        return lax.fori_loop(0, count, slot, carry)

    missed, sent = lax.fori_loop(0, PEERS, source, (jnp.int32(0), jnp.int32(0)))
    write_tags(marks, tags, counts, None, missed, GROUPS)
    tag_copy = pltpu.make_async_copy(tags, out.at[:, pl.ds(HOPS * BR, LABEL_ROWS)], tag_sem)
    tag_copy.start()

    def arrive(i, carry):
        pltpu.make_async_copy(received.at[0, pl.ds(0, BR)], staged.at[0], sem).wait()
        return carry

    def leave(k, carry):
        row = pl.multiple_of(rows[k], BR)
        pltpu.make_async_copy(staged.at[k], out.at[homes[k], pl.ds(row, BR)], sem).start()
        return carry

    def left(k, carry):
        pltpu.make_async_copy(staged.at[0], out.at[0, pl.ds(0, BR)], sem).wait()
        return carry

    lax.fori_loop(0, sent, arrive, 0)
    lax.fori_loop(0, sent, leave, 0)
    lax.fori_loop(0, sent, left, 0)
    tag_copy.wait()


def forward(index, received):
    return pl.pallas_call(
        forward_kernel,
        out_shape=jax.ShapeDtypeStruct((GROUPS, HOPS * BR + LABEL_ROWS, 128), jnp.bfloat16),
        in_specs=[
            pl.BlockSpec(memory_space=pltpu.SMEM),
            pl.BlockSpec(memory_space=pl.ANY),
        ],
        out_specs=pl.BlockSpec(memory_space=pl.ANY),
        scratch_shapes=[
            pltpu.VMEM((GROUPS, 8, 128), jnp.float32),
            pltpu.VMEM((GROUPS, LABEL_ROWS, 128), jnp.bfloat16),
            pltpu.SMEM((GROUPS,), jnp.int32),
            pltpu.VMEM((GROUPS * HOPS, BR, 128), jnp.bfloat16),
            pltpu.SMEM((GROUPS * HOPS,), jnp.int32),
            pltpu.SMEM((GROUPS * HOPS,), jnp.int32),
            pltpu.SemaphoreType.DMA,
            pltpu.SemaphoreType.DMA,
        ],
        compiler_params=pltpu.CompilerParams(vmem_limit_bytes=4 << 20),
        name="forward",
    )(index, received)


def target_of(target):
    chunk = target // OWNED
    row = target - chunk * OWNED
    return chunk, pl.multiple_of(row * BR, BR)


def direct_kernel(spot, index, received, rhs, out, total, landed, sems, sem):
    def fetch(i, at):
        def slot(j, spot):
            pltpu.make_async_copy(
                received.at[i, pl.ds(pl.multiple_of(j * BR, BR), BR)], landed.at[spot], sems.at[i]
            ).start()
            return spot + 1

        return lax.fori_loop(0, index[i, 0, COUNT_LANE], slot, at)

    lax.fori_loop(0, PEERS, fetch, jnp.int32(0))
    total[0:16] = jnp.zeros((16, CHUNK, 128), jnp.float32)
    total[spot[0], 0:PIVOT_ROWS, :] = rhs[...]

    def source(i, carry):
        missed, at = carry
        count = index[i, 0, COUNT_LANE]

        def arrive(j, carry):
            pltpu.make_async_copy(received.at[0, pl.ds(0, BR)], landed.at[0], sems.at[i]).wait()
            return carry

        lax.fori_loop(0, count, arrive, 0)

        def slot(j, spot):
            chunk, start = target_of(index[i, 0, j])
            chunk = jnp.where(index[i, 0, HOP_LANE + j] >= 0, 16, chunk)
            total[chunk, pl.ds(start, BR), :] += landed[spot].astype(jnp.float32)
            return spot + 1

        at = lax.fori_loop(0, count, slot, at)
        return missed + index[i, 0, OVER_LANE], at

    missed, _ = lax.fori_loop(0, PEERS, source, (jnp.int32(0), jnp.int32(0)))

    @pl.when(missed > 0)
    def _():
        total[0:16, 0:MARK_ROWS, :] = jnp.full((16, MARK_ROWS, 128), MARK, jnp.float32)

    copy = pltpu.make_async_copy(total.at[pl.ds(0, 16)], out, sem)
    copy.start()
    copy.wait()


def add_direct(spot, index, received, rhs):
    return pl.pallas_call(
        direct_kernel,
        out_shape=jax.ShapeDtypeStruct((16, CHUNK, 128), jnp.float32),
        in_specs=[
            pl.BlockSpec(memory_space=pltpu.SMEM),
            pl.BlockSpec(memory_space=pltpu.SMEM),
            pl.BlockSpec(memory_space=pl.ANY),
            pl.BlockSpec(memory_space=pltpu.VMEM),
        ],
        out_specs=pl.BlockSpec(memory_space=pltpu.HBM),
        scratch_shapes=[
            pltpu.VMEM((17, CHUNK, 128), jnp.float32),
            pltpu.VMEM((PEERS * SLOTS, BR, 128), jnp.bfloat16),
            pltpu.SemaphoreType.DMA((PEERS,)),
            pltpu.SemaphoreType.DMA,
        ],
        name="add_direct",
    )(spot, index, received, rhs)


def late_kernel(labels, late, dense, out, blocks, sums, flags, targets, homes, sem, sum_sem):
    def fetch(i, carry):
        def slot(j, carry):
            at, kept = carry
            target = labels[i, 0, j]

            def match(k, found):
                return jnp.where(targets[k] == target, k, found)

            found = lax.fori_loop(0, kept, match, jnp.int32(-1))
            fresh = found < 0
            homes[at] = jnp.where(fresh, kept, found)
            pltpu.make_async_copy(
                late.at[i, pl.ds(pl.multiple_of(j * BR, BR), BR)], blocks.at[at], sem
            ).start()

            @pl.when(fresh)
            def _():
                targets[kept] = target
                chunk, start = target_of(target)
                pltpu.make_async_copy(
                    dense.at[chunk, pl.ds(start, BR)], sums.at[kept], sum_sem
                ).start()

            return at + 1, kept + jnp.where(fresh, 1, 0)

        at, kept, missed = carry
        at, kept = lax.fori_loop(0, labels[i, 0, COUNT_LANE], slot, (at, kept))
        return at, kept, missed + labels[i, 0, OVER_LANE]

    zero = jnp.int32(0)
    count, kept, missed = lax.fori_loop(0, GROUPS, fetch, (zero, zero, zero))

    def arrive_block(k, carry):
        pltpu.make_async_copy(late.at[0, pl.ds(0, BR)], blocks.at[0], sem).wait()
        return carry

    def arrive_sum(k, carry):
        pltpu.make_async_copy(dense.at[0, pl.ds(0, BR)], sums.at[0], sum_sem).wait()
        return carry

    lax.fori_loop(0, count, arrive_block, 0)
    lax.fori_loop(0, kept, arrive_sum, 0)

    def add(k, carry):
        sums[homes[k]] += blocks[k].astype(jnp.float32)
        return carry

    lax.fori_loop(0, count, add, 0)

    def leave(k, carry):
        chunk, start = target_of(targets[k])
        pltpu.make_async_copy(sums.at[k], out.at[chunk, pl.ds(start, BR)], sum_sem).start()
        return carry

    def left(k, carry):
        pltpu.make_async_copy(sums.at[0], out.at[0, pl.ds(0, BR)], sum_sem).wait()
        return carry

    lax.fori_loop(0, kept, leave, 0)
    lax.fori_loop(0, kept, left, 0)

    @pl.when(missed > 0)
    def _():
        flags[...] = jnp.full(flags.shape, MARK, jnp.float32)
        mark = pltpu.make_async_copy(flags, out.at[:, pl.ds(0, MARK_ROWS)], sem)
        mark.start()
        mark.wait()


def add_late(labels, late, dense):
    most = GROUPS * HOPS
    anywhere = pl.BlockSpec(memory_space=pl.ANY)
    in_hbm = pl.BlockSpec(memory_space=pltpu.HBM)
    return pl.pallas_call(
        late_kernel,
        out_shape=jax.ShapeDtypeStruct((16, CHUNK, 128), jnp.float32),
        in_specs=[pl.BlockSpec(memory_space=pltpu.SMEM), anywhere, in_hbm],
        out_specs=in_hbm,
        input_output_aliases={2: 0},
        scratch_shapes=[
            pltpu.VMEM((most, BR, 128), jnp.bfloat16),
            pltpu.VMEM((most, BR, 128), jnp.float32),
            pltpu.VMEM((16, MARK_ROWS, 128), jnp.float32),
            pltpu.SMEM((most,), jnp.int32),
            pltpu.SMEM((most,), jnp.int32),
            pltpu.SemaphoreType.DMA,
            pltpu.SemaphoreType.DMA,
        ],
        name="add_late",
    )(labels, late, dense)


def solve_kernel(spot, pivots, rhs, *refs):
    lowers, inverses = refs[0:4], refs[4:8]
    start, update, solved_out, update_out, over, lower, inverse = refs[8:]
    marks = [rhs[block * PIVOT_ROWS : block * PIVOT_ROWS + 1, 0:128] for block in range(4)]
    highest = jnp.max(jnp.maximum(jnp.maximum(marks[0], marks[1]), jnp.maximum(marks[2], marks[3])))
    over[0] = jnp.where(highest > LIMIT, 1, 0)
    chain_at = spot[0]
    live_count = pivots[0]
    for shift in range(4):
        block = (chain_at - shift) & 3
        lower[block] = lowers[shift][...]
        inverse[block] = inverses[shift][...]
    partials = [rhs[block * PIVOT_ROWS : (block + 1) * PIVOT_ROWS, :] for block in range(4)]
    products = []
    for block in range(4):
        row = block * PIVOT_ROWS + lax.broadcasted_iota(jnp.int32, (PIVOT_ROWS, 128), 0)
        product = jnp.dot(
            inverse[block],
            partials[block],
            precision=lax.Precision.HIGHEST,
            preferred_element_type=jnp.float32,
        )
        here = jnp.where(row < live_count, product, 0.0)
        kept = here.astype(jnp.bfloat16)
        columns = slice(block * PIVOT_ROWS, (block + 1) * PIVOT_ROWS)
        for later in range(block + 1, 4):
            partials[later] = partials[later] - jnp.dot(
                lower[later, :, columns], kept, preferred_element_type=jnp.float32
            )
        products.append(jnp.dot(update[:, columns], kept, preferred_element_type=jnp.float32))

        @pl.when(chain_at == block)
        def _():
            solved_out[...] = here

    update_out[...] = start[...] - ((products[0] + products[1]) + (products[2] + products[3]))


def solve(spot, pivots, rhs, lowers, inverses, start, update):
    smem = pl.BlockSpec(memory_space=pltpu.SMEM)
    vmem = pl.BlockSpec(memory_space=pltpu.VMEM)
    return pl.pallas_call(
        solve_kernel,
        out_shape=(
            jax.ShapeDtypeStruct((PIVOT_ROWS, 128), jnp.float32),
            jax.ShapeDtypeStruct((CHUNK - PIVOT_ROWS, 128), jnp.float32),
            jax.ShapeDtypeStruct((1,), jnp.int32),
        ),
        in_specs=[smem, smem] + [vmem] * 11,
        out_specs=(vmem, vmem, smem),
        scratch_shapes=[
            pltpu.VMEM((4, PIVOT_ROWS, 3 * PIVOT_ROWS), jnp.bfloat16),
            pltpu.VMEM((4, PIVOT_ROWS, PIVOT_ROWS), jnp.float32),
        ],
        compiler_params=pltpu.CompilerParams(vmem_limit_bytes=20 << 20),
        name="solve",
    )(spot, pivots, rhs, *lowers, *inverses, start, update)


def around_chain(value):
    moved = [
        lax.ppermute(value, "chain", [(i, (i + shift) % 4) for i in range(4)])
        for shift in (1, 2, 3)
    ]
    return (value, *moved)


def labels_of(received):
    return received[:, -LABEL_ROWS : 1 - LABEL_ROWS, :].astype(jnp.int32)


def body(
    rhs, child_blocks, dest_front, dest_place, front_pivots, diag_inv, lower_factor, update_factor
):
    fronts = dest_front.reshape(-1)
    spot = lax.axis_index("chain").astype(jnp.int32).reshape(1)
    turn = lax.axis_index(LINE).astype(jnp.int32).reshape(1) + 2 * spot
    packed = pack(turn, fronts, dest_place, child_blocks)
    received = lax.all_to_all(packed, SLAB, split_axis=0, concat_axis=0, tiled=True)
    index = labels_of(received)
    late = lax.all_to_all(forward(index, received), LINE, split_axis=0, concat_axis=0, tiled=True)
    height = lax.axis_index("z").astype(jnp.int32).reshape(1)
    dense = add_late(labels_of(late), late, add_direct(height, index, received, rhs))
    dense, lower_factor, diag_inv = lax.optimization_barrier((dense, lower_factor, diag_inv))
    owned = lax.psum_scatter(dense, "z", scatter_dimension=0, tiled=True)
    lowers = around_chain(lower_factor)
    inverses = around_chain(diag_inv)
    owned, lowers, inverses = lax.optimization_barrier((owned, lowers, inverses))
    owned = owned.reshape(CHUNK, 128)

    def share(mine):
        copies = jnp.tile(mine, (4, 1))
        return lax.all_to_all(copies, "chain", split_axis=0, concat_axis=0, tiled=True)

    def finish(all_rhs, start, lowers, inverses):
        return solve(spot, front_pivots, all_rhs, lowers, inverses, start, update_factor)

    def general(*fast):
        mine = full_exchange(child_blocks, fronts, dest_place).reshape(CHUNK, 128)
        factors = around_chain(lower_factor), around_chain(diag_inv)
        all_rhs = share(rhs + mine[:PIVOT_ROWS])
        return finish(all_rhs, mine[PIVOT_ROWS:], *factors)[:2]

    all_rhs = share(owned[:PIVOT_ROWS])
    solved, updated, over = finish(all_rhs, owned[PIVOT_ROWS:], lowers, inverses)
    return lax.cond(over[0] > 0, general, lambda *fast: fast, solved, updated)


def solution(mesh):
    grid = Mesh(mesh.devices.reshape(4, 16, 2, 4), ALL)
    rows = P(ALL, None)
    return jax.shard_map(
        body,
        mesh=grid,
        in_specs=(rows, P(ALL, None, None), rows, P(ALL), P(FRONT), rows, rows, rows),
        out_specs=(rows, rows),
        check_vma=False,
    )
```

```python
import jax
import jax.numpy as jnp
from jax import lax
from jax.experimental import pallas as pl
from jax.experimental.pallas import tpu as pltpu
from jax.sharding import Mesh, PartitionSpec as P

BR = 128
FRONT = ("x", "z", "core")
ALL = ("x", "z", "core", "chain")
SLAB = ("x", "core", "chain")
LINE = ("x", "core")
SLOTS = 5
HOPS = 5
PEERS = 32
PIECES = 4
GROUPS = 8
LABEL_ROWS = 8
OWNED = 6
HOP_LANE = 64
STRAY_LANE = 125
COUNT_LANE = 126
OVER_LANE = 127
PIVOT_ROWS = 256
MARK_ROWS = 8
MARK = 1e30
LIMIT = 1e20
CHUNK = OWNED * BR


def slot_table(blocks, fronts, places, dest_count, slot_width):
    block_count = fronts.shape[0]
    sequence = jnp.arange(block_count, dtype=jnp.int32)
    earlier = (fronts[None, :] == fronts[:, None]) & (sequence[None, :] < sequence[:, None])
    rank_of = jnp.sum(earlier.astype(jnp.int32), axis=1)
    target = fronts * slot_width + rank_of
    source = jnp.full((dest_count * slot_width,), block_count, jnp.int32).at[target].set(sequence)
    slot_data = jnp.take(blocks, source, axis=0, mode="fill", fill_value=0)
    labels = jnp.take(places, source, axis=0, mode="fill", fill_value=-1)
    return (
        slot_data.reshape((dest_count, slot_width) + blocks.shape[1:]),
        labels.reshape(dest_count, slot_width),
    )


def full_exchange(child_blocks, fronts, places):
    slot_data, labels = slot_table(child_blocks, fronts, places, 128, 2)
    received = lax.all_to_all(slot_data, FRONT, split_axis=0, concat_axis=0, tiled=True)
    tags = lax.all_to_all(labels, FRONT, split_axis=0, concat_axis=0, tiled=True).reshape(-1)
    placed = jnp.where(
        tags < 8, tags // 2 * OWNED + tags % 2, (tags - 8) // 4 * OWNED + 2 + (tags - 8) % 4
    )
    placed = jnp.where(tags < 0, -1, placed)
    row_ids = jnp.arange(4 * OWNED, dtype=jnp.int32)
    onehot = (placed[None, :] == row_ids[:, None]).astype(jnp.bfloat16)
    flattened = received.reshape((-1,) + received.shape[2:])
    merged = jnp.einsum("km,mrs->krs", onehot, flattened, preferred_element_type=jnp.float32)
    return lax.psum_scatter(merged, "chain", scatter_dimension=0, tiled=True)


def write_tags(marks, tags, counts, strays, missed, count):
    lane = lax.broadcasted_iota(jnp.int32, (8, 128), 1)
    for peer in range(count):
        row = jnp.where(lane == COUNT_LANE, counts[peer].astype(jnp.float32), marks[peer])
        if strays is not None:
            row = jnp.where(lane == STRAY_LANE, strays[peer].astype(jnp.float32), row)
        row = jnp.where(lane == OVER_LANE, missed.astype(jnp.float32), row)
        tags[peer] = row.astype(jnp.bfloat16)


def send_kernel(
    spot, front, place, source, out, marks, tags, counts, strays, seen, late, slots, blocks, sem, tag_sem, in_sem
):
    piece = front.shape[0] // PIECES
    loads = [
        pltpu.make_async_copy(
            source.at[pl.ds(k * piece, piece)], blocks.at[pl.ds(k * piece, piece)], in_sem.at[k]
        )
        for k in range(PIECES)
    ]
    for load in loads:
        load.start()
    for peer in range(PEERS):
        counts[peer] = 0
        strays[peer] = 0
        seen[peer] = 0
    marks[...] = jnp.full(marks.shape, -1.0, jnp.float32)
    lane = lax.broadcasted_iota(jnp.int32, (8, 128), 1)

    def route(i):
        where_front = front[i]
        target = place[i]
        pivot = target < 8
        owner = jnp.where(pivot, target >> 1, (target - 8) >> 2)
        peer = ((where_front >> 5) * 2 + (where_front & 1)) * 4 + owner
        index = ((where_front >> 1) & 15) * OWNED + jnp.where(
            pivot, target & 1, 2 + ((target - 8) & 3)
        )
        live = target >= 0
        return live, jnp.where(live, peer, 0), index

    def launch(i, carry):
        peer = slots[i] >> 3
        used = slots[i] & 7

        @pl.when(slots[i] >= 0)
        def _():
            pltpu.make_async_copy(
                blocks.at[i], out.at[peer, pl.ds(pl.multiple_of(used * BR, BR), BR)], sem
            ).start()

        return carry

    def direct(i, carry):
        left, sent = carry
        live, peer, index = route(i)
        used = counts[peer]
        fits = live & (used < SLOTS)
        slots[i] = -1

        @pl.when(fits)
        def _():
            counts[peer] = used + 1
            slots[i] = (peer << 3) + used
            marks[peer] = jnp.where(lane == used, index.astype(jnp.float32), marks[peer])

        @pl.when(live & (used >= SLOTS))
        def _():
            late[left] = i

        return (
            left + jnp.where(live & (used >= SLOTS), 1, 0),
            sent + jnp.where(fits, 1, 0),
        )

    left, sent = lax.fori_loop(0, front.shape[0], direct, (jnp.int32(0), jnp.int32(0)))

    def detour(k, carry):
        missed, sent = carry
        i = late[k]
        _, home, index = route(i)
        group = home >> 2
        first = spot[0] + 3 * seen[home]
        seen[home] = seen[home] + 1
        chosen = jnp.int32(-1)
        for h in reversed(range(GROUPS - 1)):
            turn = lax.rem(first + h, GROUPS - 1)
            peer = (((group + 1 + turn) & 7) << 2) + (home & 3)
            chosen = jnp.where(counts[peer] < SLOTS, peer, chosen)
        fits = chosen >= 0

        @pl.when(fits)
        def _():
            used = counts[chosen]
            counts[chosen] = used + 1
            strays[chosen] = strays[chosen] + 1
            slots[i] = (chosen << 3) + used
            row = jnp.where(lane == used, index.astype(jnp.float32), marks[chosen])
            marks[chosen] = jnp.where(lane == HOP_LANE + used, group.astype(jnp.float32), row)

        return missed + jnp.where(fits, 0, 1), sent + jnp.where(fits, 1, 0)

    missed, sent = lax.fori_loop(0, left, detour, (jnp.int32(0), sent))
    for k, load in enumerate(loads):
        load.wait()
        lax.fori_loop(k * piece, (k + 1) * piece, launch, 0)
    write_tags(marks, tags, counts, strays, missed, PEERS)
    tag_copy = pltpu.make_async_copy(tags, out.at[:, pl.ds(SLOTS * BR, LABEL_ROWS)], tag_sem)
    tag_copy.start()

    def drain(i, carry):
        pltpu.make_async_copy(blocks.at[0], out.at[0, pl.ds(0, BR)], sem).wait()
        return carry

    lax.fori_loop(0, sent, drain, 0)
    tag_copy.wait()


def pack(turn, fronts, places, blocks):
    smem = pl.BlockSpec(memory_space=pltpu.SMEM)
    return pl.pallas_call(
        send_kernel,
        out_shape=jax.ShapeDtypeStruct((PEERS, SLOTS * BR + LABEL_ROWS, 128), jnp.bfloat16),
        in_specs=[smem, smem, smem, pl.BlockSpec(memory_space=pl.ANY)],
        out_specs=pl.BlockSpec(memory_space=pl.ANY),
        scratch_shapes=[
            pltpu.VMEM((PEERS, 8, 128), jnp.float32),
            pltpu.VMEM((PEERS, LABEL_ROWS, 128), jnp.bfloat16),
            pltpu.SMEM((PEERS,), jnp.int32),
            pltpu.SMEM((PEERS,), jnp.int32),
            pltpu.SMEM((PEERS,), jnp.int32),
            pltpu.SMEM((128,), jnp.int32),
            pltpu.SMEM((128,), jnp.int32),
            pltpu.VMEM(blocks.shape, jnp.bfloat16),
            pltpu.SemaphoreType.DMA,
            pltpu.SemaphoreType.DMA,
            pltpu.SemaphoreType.DMA((PIECES,)),
        ],
        name="pack",
    )(turn, fronts, places, blocks)


def forward_kernel(index, received, out, marks, tags, counts, sem, tag_sem):
    for peer in range(GROUPS):
        counts[peer] = 0
    marks[...] = jnp.full(marks.shape, -1.0, jnp.float32)
    lane = lax.broadcasted_iota(jnp.int32, (8, 128), 1)

    def source(i, carry):
        def slot(j, carry):
            missed, sent = carry
            home = index[i, 0, HOP_LANE + j]
            stray = home >= 0
            used = counts[jnp.maximum(home, 0)]
            fits = stray & (used < HOPS)

            @pl.when(fits)
            def _():
                counts[home] = used + 1
                pltpu.make_async_copy(
                    received.at[i, pl.ds(pl.multiple_of(j * BR, BR), BR)],
                    out.at[home, pl.ds(pl.multiple_of(used * BR, BR), BR)],
                    sem,
                ).start()
                target = index[i, 0, j].astype(jnp.float32)
                marks[home] = jnp.where(lane == used, target, marks[home])

            return (
                missed + jnp.where(stray & (used >= HOPS), 1, 0),
                sent + jnp.where(fits, 1, 0),
            )

        count = jnp.where(index[i, 0, STRAY_LANE] > 0, index[i, 0, COUNT_LANE], 0)
        return lax.fori_loop(0, count, slot, carry)

    missed, sent = lax.fori_loop(0, PEERS, source, (jnp.int32(0), jnp.int32(0)))
    write_tags(marks, tags, counts, None, missed, GROUPS)
    tag_copy = pltpu.make_async_copy(tags, out.at[:, pl.ds(HOPS * BR, LABEL_ROWS)], tag_sem)
    tag_copy.start()

    def drain(i, carry):
        pltpu.make_async_copy(received.at[0, pl.ds(0, BR)], out.at[0, pl.ds(0, BR)], sem).wait()
        return carry

    lax.fori_loop(0, sent, drain, 0)
    tag_copy.wait()


def forward(index, received):
    return pl.pallas_call(
        forward_kernel,
        out_shape=jax.ShapeDtypeStruct((GROUPS, HOPS * BR + LABEL_ROWS, 128), jnp.bfloat16),
        in_specs=[
            pl.BlockSpec(memory_space=pltpu.SMEM),
            pl.BlockSpec(memory_space=pl.ANY),
        ],
        out_specs=pl.BlockSpec(memory_space=pl.ANY),
        scratch_shapes=[
            pltpu.VMEM((GROUPS, 8, 128), jnp.float32),
            pltpu.VMEM((GROUPS, LABEL_ROWS, 128), jnp.bfloat16),
            pltpu.SMEM((GROUPS,), jnp.int32),
            pltpu.SemaphoreType.DMA,
            pltpu.SemaphoreType.DMA,
        ],
        compiler_params=pltpu.CompilerParams(vmem_limit_bytes=4 << 20),
        name="forward",
    )(index, received)


def target_of(target):
    chunk = target // OWNED
    row = target - chunk * OWNED
    return chunk, pl.multiple_of(row * BR, BR)


def direct_kernel(spot, index, received, rhs, out, total, landed, sems, sem):
    def fetch(i, at):
        def slot(j, spot):
            pltpu.make_async_copy(
                received.at[i, pl.ds(pl.multiple_of(j * BR, BR), BR)], landed.at[spot], sems.at[i]
            ).start()
            return spot + 1

        return lax.fori_loop(0, index[i, 0, COUNT_LANE], slot, at)

    lax.fori_loop(0, PEERS, fetch, jnp.int32(0))
    total[0:16] = jnp.zeros((16, CHUNK, 128), jnp.float32)
    total[spot[0], 0:PIVOT_ROWS, :] = rhs[...]

    def source(i, carry):
        missed, at = carry
        count = index[i, 0, COUNT_LANE]

        def arrive(j, carry):
            pltpu.make_async_copy(received.at[0, pl.ds(0, BR)], landed.at[0], sems.at[i]).wait()
            return carry

        lax.fori_loop(0, count, arrive, 0)

        def slot(j, spot):
            chunk, start = target_of(index[i, 0, j])
            chunk = jnp.where(index[i, 0, HOP_LANE + j] >= 0, 16, chunk)
            total[chunk, pl.ds(start, BR), :] += landed[spot].astype(jnp.float32)
            return spot + 1

        at = lax.fori_loop(0, count, slot, at)
        return missed + index[i, 0, OVER_LANE], at

    missed, _ = lax.fori_loop(0, PEERS, source, (jnp.int32(0), jnp.int32(0)))

    @pl.when(missed > 0)
    def _():
        total[0:16, 0:MARK_ROWS, :] = jnp.full((16, MARK_ROWS, 128), MARK, jnp.float32)

    copy = pltpu.make_async_copy(total.at[pl.ds(0, 16)], out, sem)
    copy.start()
    copy.wait()


def add_direct(spot, index, received, rhs):
    return pl.pallas_call(
        direct_kernel,
        out_shape=jax.ShapeDtypeStruct((16, CHUNK, 128), jnp.float32),
        in_specs=[
            pl.BlockSpec(memory_space=pltpu.SMEM),
            pl.BlockSpec(memory_space=pltpu.SMEM),
            pl.BlockSpec(memory_space=pl.ANY),
            pl.BlockSpec(memory_space=pltpu.VMEM),
        ],
        out_specs=pl.BlockSpec(memory_space=pltpu.HBM),
        scratch_shapes=[
            pltpu.VMEM((17, CHUNK, 128), jnp.float32),
            pltpu.VMEM((PEERS * SLOTS, BR, 128), jnp.bfloat16),
            pltpu.SemaphoreType.DMA((PEERS,)),
            pltpu.SemaphoreType.DMA,
        ],
        name="add_direct",
    )(spot, index, received, rhs)


def late_kernel(labels, late, dense, out, blocks, sums, flags, targets, homes, sem, sum_sem):
    def fetch(i, carry):
        def slot(j, carry):
            at, kept = carry
            target = labels[i, 0, j]

            def match(k, found):
                return jnp.where(targets[k] == target, k, found)

            found = lax.fori_loop(0, kept, match, jnp.int32(-1))
            fresh = found < 0
            homes[at] = jnp.where(fresh, kept, found)
            pltpu.make_async_copy(
                late.at[i, pl.ds(pl.multiple_of(j * BR, BR), BR)], blocks.at[at], sem
            ).start()

            @pl.when(fresh)
            def _():
                targets[kept] = target
                chunk, start = target_of(target)
                pltpu.make_async_copy(
                    dense.at[chunk, pl.ds(start, BR)], sums.at[kept], sum_sem
                ).start()

            return at + 1, kept + jnp.where(fresh, 1, 0)

        at, kept, missed = carry
        at, kept = lax.fori_loop(0, labels[i, 0, COUNT_LANE], slot, (at, kept))
        return at, kept, missed + labels[i, 0, OVER_LANE]

    zero = jnp.int32(0)
    count, kept, missed = lax.fori_loop(0, GROUPS, fetch, (zero, zero, zero))

    def arrive_block(k, carry):
        pltpu.make_async_copy(late.at[0, pl.ds(0, BR)], blocks.at[0], sem).wait()
        return carry

    def arrive_sum(k, carry):
        pltpu.make_async_copy(dense.at[0, pl.ds(0, BR)], sums.at[0], sum_sem).wait()
        return carry

    lax.fori_loop(0, count, arrive_block, 0)
    lax.fori_loop(0, kept, arrive_sum, 0)

    def add(k, carry):
        sums[homes[k]] += blocks[k].astype(jnp.float32)
        return carry

    lax.fori_loop(0, count, add, 0)

    def leave(k, carry):
        chunk, start = target_of(targets[k])
        pltpu.make_async_copy(sums.at[k], out.at[chunk, pl.ds(start, BR)], sum_sem).start()
        return carry

    def left(k, carry):
        pltpu.make_async_copy(sums.at[0], out.at[0, pl.ds(0, BR)], sum_sem).wait()
        return carry

    lax.fori_loop(0, kept, leave, 0)
    lax.fori_loop(0, kept, left, 0)

    @pl.when(missed > 0)
    def _():
        flags[...] = jnp.full(flags.shape, MARK, jnp.float32)
        mark = pltpu.make_async_copy(flags, out.at[:, pl.ds(0, MARK_ROWS)], sem)
        mark.start()
        mark.wait()


def add_late(labels, late, dense):
    most = GROUPS * HOPS
    anywhere = pl.BlockSpec(memory_space=pl.ANY)
    in_hbm = pl.BlockSpec(memory_space=pltpu.HBM)
    return pl.pallas_call(
        late_kernel,
        out_shape=jax.ShapeDtypeStruct((16, CHUNK, 128), jnp.float32),
        in_specs=[pl.BlockSpec(memory_space=pltpu.SMEM), anywhere, in_hbm],
        out_specs=in_hbm,
        input_output_aliases={2: 0},
        scratch_shapes=[
            pltpu.VMEM((most, BR, 128), jnp.bfloat16),
            pltpu.VMEM((most, BR, 128), jnp.float32),
            pltpu.VMEM((16, MARK_ROWS, 128), jnp.float32),
            pltpu.SMEM((most,), jnp.int32),
            pltpu.SMEM((most,), jnp.int32),
            pltpu.SemaphoreType.DMA,
            pltpu.SemaphoreType.DMA,
        ],
        name="add_late",
    )(labels, late, dense)


def solve_kernel(spot, pivots, rhs, *refs):
    lowers, inverses = refs[0:4], refs[4:8]
    start, update, solved_out, update_out, over, lower, inverse = refs[8:]
    marks = [rhs[block * PIVOT_ROWS : block * PIVOT_ROWS + 1, 0:128] for block in range(4)]
    highest = jnp.max(jnp.maximum(jnp.maximum(marks[0], marks[1]), jnp.maximum(marks[2], marks[3])))
    over[0] = jnp.where(highest > LIMIT, 1, 0)
    chain_at = spot[0]
    live_count = pivots[0]
    for shift in range(4):
        block = (chain_at - shift) & 3
        lower[block] = lowers[shift][...]
        inverse[block] = inverses[shift][...]
    partials = [rhs[block * PIVOT_ROWS : (block + 1) * PIVOT_ROWS, :] for block in range(4)]
    products = []
    for block in range(4):
        row = block * PIVOT_ROWS + lax.broadcasted_iota(jnp.int32, (PIVOT_ROWS, 128), 0)
        product = jnp.dot(
            inverse[block],
            partials[block],
            precision=lax.Precision.HIGHEST,
            preferred_element_type=jnp.float32,
        )
        here = jnp.where(row < live_count, product, 0.0)
        kept = here.astype(jnp.bfloat16)
        columns = slice(block * PIVOT_ROWS, (block + 1) * PIVOT_ROWS)
        for later in range(block + 1, 4):
            partials[later] = partials[later] - jnp.dot(
                lower[later, :, columns], kept, preferred_element_type=jnp.float32
            )
        products.append(jnp.dot(update[:, columns], kept, preferred_element_type=jnp.float32))

        @pl.when(chain_at == block)
        def _():
            solved_out[...] = here

    update_out[...] = start[...] - ((products[0] + products[1]) + (products[2] + products[3]))


def solve(spot, pivots, rhs, lowers, inverses, start, update):
    smem = pl.BlockSpec(memory_space=pltpu.SMEM)
    vmem = pl.BlockSpec(memory_space=pltpu.VMEM)
    return pl.pallas_call(
        solve_kernel,
        out_shape=(
            jax.ShapeDtypeStruct((PIVOT_ROWS, 128), jnp.float32),
            jax.ShapeDtypeStruct((CHUNK - PIVOT_ROWS, 128), jnp.float32),
            jax.ShapeDtypeStruct((1,), jnp.int32),
        ),
        in_specs=[smem, smem] + [vmem] * 11,
        out_specs=(vmem, vmem, smem),
        scratch_shapes=[
            pltpu.VMEM((4, PIVOT_ROWS, 3 * PIVOT_ROWS), jnp.bfloat16),
            pltpu.VMEM((4, PIVOT_ROWS, PIVOT_ROWS), jnp.float32),
        ],
        compiler_params=pltpu.CompilerParams(vmem_limit_bytes=20 << 20),
        name="solve",
    )(spot, pivots, rhs, *lowers, *inverses, start, update)


def around_chain(value):
    moved = [
        lax.ppermute(value, "chain", [(i, (i + shift) % 4) for i in range(4)])
        for shift in (1, 2, 3)
    ]
    return (value, *moved)


def labels_of(received):
    return received[:, -LABEL_ROWS : 1 - LABEL_ROWS, :].astype(jnp.int32)


def body(
    rhs, child_blocks, dest_front, dest_place, front_pivots, diag_inv, lower_factor, update_factor
):
    fronts = dest_front.reshape(-1)
    spot = lax.axis_index("chain").astype(jnp.int32).reshape(1)
    turn = lax.axis_index(LINE).astype(jnp.int32).reshape(1) + 2 * spot
    packed = pack(turn, fronts, dest_place, child_blocks)
    received = lax.all_to_all(packed, SLAB, split_axis=0, concat_axis=0, tiled=True)
    index = labels_of(received)
    late = lax.all_to_all(forward(index, received), LINE, split_axis=0, concat_axis=0, tiled=True)
    height = lax.axis_index("z").astype(jnp.int32).reshape(1)
    dense = add_late(labels_of(late), late, add_direct(height, index, received, rhs))
    dense, lower_factor, diag_inv = lax.optimization_barrier((dense, lower_factor, diag_inv))
    owned = lax.psum_scatter(dense, "z", scatter_dimension=0, tiled=True)
    lowers = around_chain(lower_factor)
    inverses = around_chain(diag_inv)
    owned, lowers, inverses = lax.optimization_barrier((owned, lowers, inverses))
    owned = owned.reshape(CHUNK, 128)

    def share(mine):
        copies = jnp.tile(mine, (4, 1))
        return lax.all_to_all(copies, "chain", split_axis=0, concat_axis=0, tiled=True)

    def finish(all_rhs, start, lowers, inverses):
        return solve(spot, front_pivots, all_rhs, lowers, inverses, start, update_factor)

    def general(*fast):
        mine = full_exchange(child_blocks, fronts, dest_place).reshape(CHUNK, 128)
        factors = around_chain(lower_factor), around_chain(diag_inv)
        all_rhs = share(rhs + mine[:PIVOT_ROWS])
        return finish(all_rhs, mine[PIVOT_ROWS:], *factors)[:2]

    all_rhs = share(owned[:PIVOT_ROWS])
    solved, updated, over = finish(all_rhs, owned[PIVOT_ROWS:], lowers, inverses)
    return lax.cond(over[0] > 0, general, lambda *fast: fast, solved, updated)


def solution(mesh):
    grid = Mesh(mesh.devices.reshape(4, 16, 2, 4), ALL)
    rows = P(ALL, None)
    return jax.shard_map(
        body,
        mesh=grid,
        in_specs=(rows, P(ALL, None, None), rows, P(ALL), P(FRONT), rows, rows, rows),
        out_specs=(rows, rows),
        check_vma=False,
    )
```
